32 devices in a mesh: batch: 4 (over x, core), centers: 8 (over z, y).
Axes of the slice: x: 2, y: 2, z: 4, core: 2. Of those that a mesh axis runs over, the one named last changes fastest.
Arguments:
- pool_features: float32 [32768, 128], P(('batch', 'centers')), may hold values from -14 to 14
- pool_targets: float32 [32768, 64], P(('batch', 'centers')), may hold values from -6 to 6
- batch_index: int32 [2048], P(('batch', 'centers')), may hold values from 0 to 1023
- centers: float32 [4096, 128], P('centers'), may hold values from -14 to 14
- weights: float32 [4096, 64], P('centers'), as said below
- eig_vectors: float32 [4096, 1024], P(('batch', 'centers')), may hold values from -0.09375 to 0.09375
- eig_scale: float32 [1024], replicated, may hold values from 0.5 to 4
- nys_owner: int32 [4096, 1], P(('batch', 'centers')), may hold values from 0 to 7; in each aligned block of 128 rows (0 to 127, 128 to 255, ...) at most 32 rows name the same one
- nys_offset: int32 [4096], P(('batch', 'centers')), may hold values from 0 to 511
Outputs:
- residual_out: float32 [2048, 64], P(('batch', 'centers'))
- update: float32 [4096, 64], P('centers')
The draws below stay inside these ranges and needn't reach their ends.
Inputs may be any that keep to these rules, and one draw needn't show every extreme that they name: `nys_owner`: among the 128 rows of one device no owner is named more than 32 times; on some devices one owner is named exactly 32 times. `weights`: every column sums to zero.
All inputs are finite; a program needn't handle non-finite values.
Results may differ from the reference program's by a relative error of at most 0.0003.
Values sent between devices are 32-bit elements; how exact they have to be, the bound alone decides.
A program may use at most 64 MiB of HBM per device.

```python
import math
import jax
import jax.numpy as jnp
import numpy as np
from jax import lax

D = 128
OUT = 64
Q = 1024
DEPTH = 3
NYS_DEV = 128
POOL_DEV = 1024
ROWS_LOC = 64
CDEV = 512
CAP = 32
M = 2048
P_SIZE = 4096
S = 4096
POOL = 32768
N_CENTERS = 8


def cluster_means(key):
    means = jax.random.truncated_normal(jax.random.fold_in(key, 101), -4.0, 4.0, (16, D), jnp.float32)
    return means


def noisy_points(key, count, salt):
    means = cluster_means(key)
    label = jax.random.randint(jax.random.fold_in(key, salt), (count,), 0, means.shape[0])
    level = jnp.exp(jax.random.uniform(jax.random.fold_in(key, salt + 1), (count, 1), jnp.float32, math.log(0.15), math.log(2.0)))
    noise = jax.random.truncated_normal(jax.random.fold_in(key, salt + 2), -4.0, 4.0, (count, D), jnp.float32)
    return means[label] + level * noise


def draw_pool_features(key, part):
    return noisy_points(key, POOL, 301)


def draw_centers(key, part):
    return noisy_points(key, P_SIZE, 401)


def draw_weights(key, part):
    base = jax.random.normal(jax.random.fold_in(key, 501), (P_SIZE, OUT), jnp.float32)
    base = base - jnp.mean(base, axis=0, keepdims=True)
    return base * (0.3 / math.sqrt(P_SIZE))


def set_ends(values, rng, smallest, high):
    longest = values.shape.index(max(values.shape))
    spots = []
    for shift in (0, 1):
        where = [jax.random.randint(jax.random.fold_in(rng, axis), (), 0, length) for axis, length in enumerate(values.shape)]
        where[longest] = (where[longest] + shift) % values.shape[longest]
        spots.append(tuple(where))
    return values.at[spots[0]].set(smallest).at[spots[1]].set(high)


def steps_of(stream_key, extent, shards, low, largest):
    factor_of, own = 1.0, jax.random.fold_in(stream_key, 6)
    for position, blocks in shards:
        draws = jnp.exp(jax.random.uniform(jax.random.fold_in(own, position), (blocks,), jnp.float32, low / len(shards), largest / len(shards)))
        factor_of = factor_of * jnp.repeat(draws, extent[position] // blocks).reshape([-1 if axis == position else 1 for axis in range(len(extent))])
    return factor_of


def routed_block(own_key, own, number, rows, number_of, top, bound, slope):
    sequence = jax.random.permutation(own_key, number_of)
    crowded, common = load_shares(number_of, rows * top, bound, slope, True), load_shares(number_of, rows * top, bound, slope, False)
    places = jnp.arange(number_of)

    def named(lengths, turn):
        used = int((lengths > 0).sum())
        fixed = max(1, used // 4)
        moved = fixed + (places - fixed + turn * (used - fixed)) % max(1, number_of - fixed)
        return jnp.zeros((number_of,), jnp.int32).at[sequence[jnp.where(places < fixed, places, moved)]].set(jnp.asarray(lengths, jnp.int32))

    lengths = jnp.where(number % 4 == 0, named(crowded, number // 4), named(common, number - number // 4 - 1))
    mixed = jax.random.permutation(jax.random.fold_in(own, 3), number_of)
    donor, receiver = mixed[0:number_of // 2 * 2:2], mixed[1:number_of // 2 * 2:2]
    slack = jnp.minimum(lengths[donor] - 1, bound - lengths[receiver]) // 2
    slack = jnp.where((donor == sequence[0]) | (receiver == sequence[0]) | (lengths[receiver] == 0), 0, jnp.maximum(slack, 0))
    moved = jax.random.randint(jax.random.fold_in(own, 4), (number_of // 2,), 0, 1 << 20) % (slack + 1)
    lengths = lengths.at[donor].add(-moved).at[receiver].add(moved)
    members = jnp.searchsorted(jnp.cumsum(lengths), jnp.arange(rows * top), side="right").astype(jnp.int32)
    listing = members.reshape(top, rows).T
    listing = listing[jax.random.permutation(jax.random.fold_in(own, 1), rows)]
    turn = jax.random.randint(jax.random.fold_in(own, 2), (rows, 1), 0, top)
    return jnp.take_along_axis(listing, (jnp.arange(top)[None, :] + turn) % top, axis=1)


def load_shares(number_of, total, reach, lean, full):
    weights = [(1 << 20) // math.isqrt(standing ** lean) + 1 for standing in range(1, number_of + 1)]
    largest = reach if full else min(reach, max(-(-total // number_of), total * weights[0] // sum(weights)))
    least = 1 if total - largest >= number_of - 1 else 0
    holding, surplus = [largest] + [least] * (number_of - 1), total - largest - least * (number_of - 1)
    while surplus > 0:
        movable = [i for i in range(1, number_of) if holding[i] < largest] or [i for i in range(1, number_of) if holding[i] < reach]
        whole, left = sum([weights[i] for i in movable]), surplus
        for i in movable:
            extra = min(reach - holding[i], max(1, left * weights[i] // whole), surplus)
            holding[i] = holding[i] + extra
            surplus = surplus - extra
    return np.array(holding)


def normal_values(stream_key, shape, deviation, bound, cuts=(), kind=jnp.bfloat16):
    values = jax.random.normal(stream_key, shape, jnp.float32) * deviation
    if len(cuts) > 0:
        values = steps_of(stream_key, shape, cuts, -0.22, 0.18) * values
    return jnp.clip(values, min=-bound, max=bound).astype(kind)


def setup_inputs(seed: int = 0) -> dict:
    key_list = jax.random.split(jax.random.key(seed), 10)
    pool_features = draw_pool_features(jax.random.fold_in(key_list[9], 71), 0)
    pool_targets = normal_values(key_list[1], (POOL, OUT), 1.0, 6.0, ((0, 32),), jnp.float32)
    batch_index = set_ends(jax.random.randint(key_list[2], (M,), 0, POOL_DEV), jax.random.fold_in(key_list[2], 1), 0, POOL_DEV - 1).astype(jnp.int32)
    centers = draw_centers(jax.random.fold_in(key_list[9], 71), 0)
    weights = draw_weights(jax.random.fold_in(key_list[9], 71), 0)
    eig_vectors = normal_values(key_list[5], (S, Q), S ** -0.5, 0.09375, ((0, 32),), jnp.float32)
    eig_scale = jnp.clip(jnp.exp(jax.random.uniform(key_list[6], (Q,), jnp.float32, math.log(0.5), math.log(4.0))), 0.5, 4.0)
    nys_owner_keys = jax.random.split(jax.random.fold_in(key_list[7], 1), S // NYS_DEV)
    nys_owner_turns = jax.random.permutation(jax.random.fold_in(key_list[7], 3), S // NYS_DEV)
    nys_owner = jax.vmap(lambda own, number: routed_block(jax.random.fold_in(key_list[7], 2), own, number, NYS_DEV, N_CENTERS, 1, CAP, 2))(nys_owner_keys, nys_owner_turns).reshape((S, 1))
    nys_offset = set_ends(jax.random.randint(key_list[8], (S,), 0, CDEV), jax.random.fold_in(key_list[8], 1), 0, CDEV - 1).astype(jnp.int32)
    return {"pool_features": pool_features, "pool_targets": pool_targets, "batch_index": batch_index, "centers": centers, "weights": weights, "eig_vectors": eig_vectors, "eig_scale": eig_scale, "nys_owner": nys_owner, "nys_offset": nys_offset}


epsilon = 1e-06
highest = lax.Precision.HIGHEST

def kernel_rows(row_block, center_block, center_norm):
    inner_prod = lax.dot_general(row_block, center_block, (((1,), (1,)), ((), ())), precision=highest, preferred_element_type=jnp.float32) / row_block.shape[1]
    row_norm = lax.optimization_barrier(jnp.mean(row_block * row_block, axis=1)) + epsilon
    norm_scale = jnp.sqrt(row_norm[:, None] * center_norm[None, :])
    sigma_now = inner_prod
    tangent = inner_prod
    for depth_step in range(DEPTH):
        cosine = sigma_now / norm_scale
        arc_angle = jnp.arccos(cosine)
        remain = (math.pi - arc_angle) / math.pi
        sigma_now = norm_scale * (jnp.sqrt(1.0 - cosine * cosine) + (math.pi - arc_angle) * cosine) / math.pi
        tangent = sigma_now + tangent * remain
    return tangent

def reference(pool_features, pool_targets, batch_index, centers, weights, eig_vectors, eig_scale, nys_owner, nys_offset):
    rows_total = batch_index.shape[0]
    block_of = jnp.arange(rows_total, dtype=jnp.int32) // ROWS_LOC
    picked = (block_of * POOL_DEV + batch_index).astype(jnp.int32)
    features = pool_features[picked]
    targets = pool_targets[picked]
    center_norm = lax.optimization_barrier(jnp.mean(centers * centers, axis=1)) + epsilon
    block_size = math.gcd(512, rows_total)
    block_count = rows_total // block_size
    feat_blocks = features.reshape(block_count, block_size, features.shape[1])
    targ_blocks = targets.reshape(block_count, block_size, targets.shape[1])

    def step_block(accum, pieces):
        feat, targ = pieces
        kern = kernel_rows(feat, centers, center_norm)
        pred = jnp.dot(kern, weights, precision=highest, preferred_element_type=jnp.float32)
        resid = pred - targ
        accum = accum + lax.dot_general(kern, resid, (((0,), (0,)), ((), ())), precision=highest, preferred_element_type=jnp.float32)
        return (accum, resid)
    total, resid_blocks = lax.scan(step_block, jnp.zeros((centers.shape[0], weights.shape[1]), jnp.float32), (feat_blocks, targ_blocks))
    residual_out = resid_blocks.reshape(rows_total, weights.shape[1])
    grads = total / math.sqrt(rows_total)
    nys = (nys_owner[:, 0] * CDEV + nys_offset).astype(jnp.int32)
    coeff = lax.dot_general(eig_vectors, grads[nys], (((0,), (0,)), ((), ())), precision=highest, preferred_element_type=jnp.float32)
    corr_rows = jnp.dot(eig_vectors, eig_scale[:, None] * coeff, precision=highest, preferred_element_type=jnp.float32)
    correction = jnp.zeros((centers.shape[0], weights.shape[1]), jnp.float32).at[nys].add(corr_rows)
    return (residual_out, correction - grads)
```

```python
import functools
import math

import jax
import jax.numpy as jnp
from jax import lax
from jax.experimental import pallas as pl
from jax.experimental.pallas import tpu as pltpu
from jax.sharding import PartitionSpec as P

DEPTH = 3
EPS = 1e-06
HIGH = lax.Precision.HIGHEST
MESH = pl.DeviceIdType.MESH
LOW = jnp.bfloat16
F32 = jnp.float32
FAR = (2, 1, 1, 1, 0)
NEAR = (0, 2, 2, 2, 2)
ACOS = (
    1.5707963050,
    -0.2145988016,
    0.0889789874,
    -0.0501743046,
    0.0308918810,
    -0.0170881256,
    0.0066700901,
    -0.0012624911,
)


def dot(a, b, ca, cb):
    return lax.dot_general(a, b, (((ca,), (cb,)), ((), ())), preferred_element_type=F32)


def exact(a, b, ca, cb):
    return lax.dot_general(
        a, b, (((ca,), (cb,)), ((), ())), precision=HIGH, preferred_element_type=F32
    )


def split(x):
    hi = x.astype(LOW)
    return hi, (x - hi.astype(F32)).astype(LOW)


def dot3(a, b, ca, cb):
    (ah, al), (bh, bl) = a, b
    rows = ah.shape[1 - ca]
    both = dot(jnp.concatenate([ah, al], axis=1 - ca), bh, ca, cb)
    return both[:rows] + both[rows:] + dot(ah, bl, ca, cb)


def fold(x):
    h = x.shape[0] // 2
    return jnp.concatenate([x[:h], x[h:]], axis=1)


def unfold(x):
    h = x.shape[1] // 2
    return jnp.concatenate([x[:, :h], x[:, h:]], axis=0)


def arc_parts(x):
    u = jnp.maximum(1.0 - x, 1e-30)
    poly = jnp.full_like(x, ACOS[-1] / math.pi)
    for a in ACOS[-2::-1]:
        poly = poly * x + a / math.pi
    v = u * (1.0 + x)
    return u * lax.rsqrt(u) * poly, v * lax.rsqrt(v) * (1.0 / math.pi)


def tangent_kernel(cosine):
    arc, sine = arc_parts(jnp.abs(cosine))
    remain = jnp.where(cosine < 0.0, arc, 1.0 - arc)
    prod = remain * cosine
    sigma = sine + prod
    tangent = sigma + prod
    for _ in range(DEPTH - 1):
        arc, sine = arc_parts(sigma)
        remain = 1.0 - arc
        sigma = sine + remain * sigma
        tangent = sigma + tangent * remain
    return tangent


def body(
    nb,
    nc,
    pool_f_h,
    pool_t_h,
    index_h,
    cen_h,
    wts_h,
    eig_h,
    scale_h,
    owner_h,
    offset_h,
    res_out,
    upd_out,
    pool_f,
    pool_t,
    index,
    index_s,
    cen,
    wts,
    eig,
    scale,
    owner,
    offset,
    res_v,
    upd_v,
    feat,
    feat_all,
    ccat,
    wcat,
    kh,
    kl,
    ppart,
    prx,
    rsend,
    rrx,
    packed,
    eigrx,
    offsend,
    offrx,
    ebar,
    gsend,
    grx,
    gown,
    gxrx,
    gall,
    csend,
    crx,
    cown,
    call,
    usend,
    urx,
    uown,
    uxrx,
    uall,
    in_s,
    out_s,
    f_s,
    f_r,
    p_s,
    p_r,
    r_s,
    r_r,
    e_s,
    e_r,
    o_s,
    o_r,
    g_s,
    g_r,
    c_s,
    c_r,
    ca_s,
    ca_r,
    u_s,
    u_r,
):
    b = lax.axis_index("batch")
    c = lax.axis_index("centers")
    n = nb * nc
    me = b * nc + c
    half = nb // 2
    k2, x = lax.rem(b, 2), lax.div(b, 2)
    z, y = lax.div(c, 2), lax.rem(c, 2)
    nz = nc // 2
    mine = c * nb + b
    rows, dim = feat.shape
    outs, cdev = wts.shape
    pts = owner.shape[1]
    group = 2 * nb
    slots = packed.shape[1] // nc
    qb = packed.shape[2]
    piece = cdev // 4
    rows_total = rows * n

    def copy(src, dst, ssem, rsem, db, dc):
        return pltpu.make_async_remote_copy(
            src_ref=src,
            dst_ref=dst,
            send_sem=ssem,
            recv_sem=rsem,
            device_id=(db, dc),
            device_id_type=MESH,
        )

    barrier = pltpu.get_barrier_semaphore()

    @pl.loop(1, n)
    def _(k):
        d = lax.rem(me + k, n)
        pl.semaphore_signal(
            barrier, inc=1, device_id=(lax.div(d, nc), lax.rem(d, nc)), device_id_type=MESH
        )

    loads = [
        pltpu.make_async_copy(src, dst, in_s.at[i])
        for i, (src, dst) in enumerate(
            (
                (index_h, index_s),
                (pool_f_h, pool_f),
                (owner_h, owner),
                (offset_h, offset),
                (eig_h, eig),
                (cen_h, cen),
                (wts_h, wts),
                (scale_h, scale),
                (index_h, index),
                (pool_t_h, pool_t),
            )
        )
    ]
    for load in loads:
        load.start()

    loads[0].wait()
    loads[1].wait()

    @pl.loop(0, rows, unroll=8)
    def _(j):
        feat[pl.ds(j, 1), :] = pool_f[pl.ds(index_s[0, j], 1), :]

    feat_all[c] = feat[...]

    loads[2].wait()
    loads[3].wait()
    own = owner[...]
    hot = (own == lax.broadcasted_iota(jnp.int32, (nc, pts), 0)).astype(F32)
    upper = (
        lax.broadcasted_iota(jnp.int32, (pts, pts), 0)
        < lax.broadcasted_iota(jnp.int32, (pts, pts), 1)
    ).astype(F32)
    rank = jnp.sum(
        dot(hot.astype(LOW), upper.astype(LOW), 1, 0) * hot, axis=0, keepdims=True
    ).astype(jnp.int32)
    place = (
        (lax.broadcasted_iota(jnp.int32, (nc * slots, pts), 0) == own * slots + rank)
        .astype(F32)
        .astype(LOW)
    )
    loads[4].wait()
    both = jnp.concatenate(split(eig[...]), axis=0)
    place2 = jnp.concatenate([place, place], axis=1)
    for j in range(nb):
        packed[j] = dot(place2, both[:, j * qb : (j + 1) * qb], 1, 0)
    here = (
        lax.broadcasted_iota(jnp.int32, (group * slots, pts), 0)
        == (y * nb + b) * slots + rank
    ).astype(F32)
    marks = exact(hot * (offset[...].astype(F32) + 1.0), here, 1, 1)
    for j in range(nc):
        offsend[j] = marks[j : j + 1]
    eigrx[mine] = packed[b, pl.ds(pl.multiple_of(c * slots, slots), slots)]
    offrx[mine] = offsend[c]

    loads[5].wait()
    cval = cen[...]
    csq = cval * cval
    ncol = jnp.mean(csq, axis=1, keepdims=True) + EPS
    ch, cl = split(cval / (jnp.sqrt(ncol) * dim))
    ccat[...] = jnp.concatenate([ch, cl, ch, cl], axis=1)
    sb_row = jnp.sqrt(exact(jnp.full((8, dim), 1.0 / dim, F32), csq, 1, 1)[0:1] + EPS)
    loads[6].wait()
    wcat[...] = jnp.concatenate(split(wts[...] * sb_row), axis=0)

    pl.semaphore_wait(barrier, n - 1)

    def at(zo, yo):
        return (z ^ zo) * 2 + (y ^ yo)

    def f_copy(t):
        d = at(lax.div(t, 2), lax.rem(t, 2))
        return copy(feat, feat_all.at[c], f_s.at[t], f_r.at[c], b, d)

    def f_wait(t):
        s = at(lax.div(t, 2), lax.rem(t, 2))
        copy(feat, feat_all.at[s], f_s.at[t], f_r.at[s], b, s).wait_recv()

    @pl.loop(1, nc)
    def _(t):
        f_copy(nc - t).start()

    def e_place(t):
        o = n - 1 - t
        return lax.rem(b + lax.rem(o, nb), nb), at(lax.div(o, group), lax.rem(lax.div(o, nb), 2))

    def e_source(o):
        return lax.rem(b - lax.rem(o, nb) + nb, nb), at(
            lax.div(o, group), lax.rem(lax.div(o, nb), 2)
        )

    def e_copy(t):
        db, dc = e_place(t)
        return copy(
            packed.at[db, pl.ds(pl.multiple_of(dc * slots, slots), slots)],
            eigrx.at[mine],
            e_s.at[t],
            e_r.at[mine],
            db,
            dc,
        )

    def o_copy(t):
        db, dc = e_place(t)
        return copy(offsend.at[dc], offrx.at[mine], o_s.at[t], o_r.at[mine], db, dc)

    marks_at = [0, n // 2]
    ends_at = [n // 2, n - 1]

    def e_start(step):
        for kind, plan in enumerate((FAR, NEAR)):
            lo, total = marks_at[kind], ends_at[kind]
            hi = total if step == len(plan) - 1 else min(total, lo + plan[step] * n // 16)
            marks_at[kind] = hi

            @pl.loop(lo, hi)
            def _(t):
                e_copy(t).start()

    e_start(0)

    def p_copy(t):
        s = at(lax.div(t, 2), lax.rem(t, 2))
        return copy(ppart.at[s], prx.at[c], p_s.at[t], p_r.at[c], b, s)

    def pair(p):
        zs = z ^ p
        av = feat_all[pl.ds(zs * 2, 2)].reshape(2 * rows, dim)
        na = jnp.mean(av * av, axis=1, keepdims=True) + EPS
        ah, al = split(av * lax.rsqrt(na))
        k = tangent_kernel(dot(jnp.concatenate([ah, ah, al, al], axis=1), ccat[...], 1, 1))
        hi, lo = split(k)
        kh[zs] = hi
        kl[zs] = lo
        top = dot(hi, wcat[...], 1, 1)
        pred = top[:, :outs] + top[:, outs:] + dot(lo, wcat[:outs], 1, 1)
        return fold(pred[:rows]), fold(pred[rows:])

    f_wait(1)
    low, high = pair(0)
    prx[c] = jnp.where(y == 0, low, high)
    ppart[c ^ 1] = jnp.where(y == 0, high, low)
    p_copy(1).start()
    e_start(1)

    def later(p):
        f_wait(2 * p)
        f_wait(2 * p + 1)
        lo, hi = pair(p)
        zs = (z ^ p) * 2
        ppart[zs] = lo
        ppart[zs + 1] = hi
        p_copy(2 * p).start()
        p_copy(2 * p + 1).start()

    for p in range(1, 3):
        later(p)
        e_start(p + 1)

    @pl.loop(3, nz)
    def _(p):
        later(p)

    a = feat[...]
    sa = jnp.sqrt(jnp.mean(a * a, axis=1, keepdims=True) + EPS)
    loads[7].wait()
    loads[8].wait()
    loads[9].wait()
    drawn = (
        (lax.broadcasted_iota(jnp.int32, (pool_t.shape[1], rows), 0) == index[...])
        .astype(F32)
        .astype(LOW)
    )
    th, tl = split(pool_t[...])
    picked = dot(jnp.concatenate([th, tl], axis=0), drawn, 1, 0)
    targ = (picked[:outs] + picked[outs:]).T

    @pl.loop(1, nc)
    def _(t):
        s = at(lax.div(t, 2), lax.rem(t, 2))
        copy(ppart.at[s], prx.at[s], p_s.at[t], p_r.at[s], b, s).wait_recv()

    pred = prx[0]
    for j in range(1, nc):
        pred = pred + prx[j]
    resid = unfold(pred) * sa - targ
    folded = fold(resid * (sa / math.sqrt(rows_total)))
    rsend[...] = folded
    rrx[c] = folded

    def r_copy(t):
        return copy(
            rsend, rrx.at[c], r_s.at[t], r_r.at[c], b, at(lax.div(t, 2), lax.rem(t, 2))
        )

    @pl.loop(1, nc)
    def _(t):
        r_copy(nc - t).start()

    @pl.loop(0, n - 1)
    def _(t):
        o_copy(t).start()

    e_start(4)

    res_v[...] = resid
    res_store = pltpu.make_async_copy(res_v, res_out, out_s.at[0])
    res_store.start()

    @pl.loop(1, nc)
    def _(t):
        s = at(lax.div(t, 2), lax.rem(t, 2))
        copy(rsend, rrx.at[s], r_s.at[t], r_r.at[s], b, s).wait_recv()

    every = jnp.concatenate([unfold(rrx[j]) for j in range(nc)], axis=0)
    eh, el = split(every)
    khv = kh[...].reshape(nc * rows, cdev)
    up = dot(jnp.concatenate([eh, el], axis=1), khv, 0, 0)
    gt = (
        up[:outs] + up[outs:] + dot(eh, kl[...].reshape(nc * rows, cdev), 0, 0)
    ) * sb_row

    def reduce_parts(part, send, rx, owned, xrx, full, ssem, rsem):
        mate = b + 1 - 2 * k2
        started = []
        for j in range(4):
            send[j] = part[:, j * piece : (j + 1) * piece]
        away = copy(
            send.at[pl.ds(2 * (1 - k2), 2)], rx, ssem.at[0], rsem.at[0], mate, c
        )
        away.start()
        started.append(away)
        yield
        away.wait_recv()
        owned[...] = send[pl.ds(2 * k2, 2)] + rx[...]
        for i in range(1, half):
            d = lax.rem(x + i, half) * 2 + k2
            out = copy(owned, xrx.at[x], ssem.at[i], rsem.at[1 + x], d, c)
            out.start()
            started.append(out)
        yield
        total = owned[...]
        for i in range(1, half):
            s = lax.rem(x + i, half)
            copy(owned, xrx.at[s], ssem.at[i], rsem.at[1 + s], s * 2 + k2, c).wait_recv()
            total = total + xrx[s]
        full[pl.ds(2 * k2, 2)] = total
        across = copy(
            full.at[pl.ds(2 * k2, 2)],
            full.at[pl.ds(2 * k2, 2)],
            ssem.at[half],
            rsem.at[1 + half],
            mate,
            c,
        )
        across.start()
        started.append(across)
        yield
        copy(
            full.at[pl.ds(2 * k2, 2)],
            full.at[pl.ds(2 * (1 - k2), 2)],
            ssem.at[half],
            rsem.at[1 + half],
            mate,
            c,
        ).wait_recv()
        yield
        for s in started:
            s.wait_send()
        yield

    def add_group(p):
        zs = z ^ p
        base = zs * group

        @pl.loop(1 if p == 0 else 0, group)
        def _(i):
            sb, sc = e_source(p * group + i)
            s = sc * nb + sb
            t = n - 1 - (p * group + i)
            copy(offsend.at[0], offrx.at[s], o_s.at[t], o_r.at[s], b, c).wait_recv()
            copy(packed.at[0, pl.ds(0, slots)], eigrx.at[s], e_s.at[t], e_r.at[s], b, c).wait_recv()

        mark = offrx[base]
        for i in range(1, group):
            mark = mark + offrx[base + i]
        sel = (
            (
                lax.broadcasted_iota(jnp.int32, (cdev, group * slots), 0) + 1
                == mark.astype(jnp.int32)
            )
            .astype(F32)
            .astype(LOW)
        )
        parts = split(eigrx[pl.ds(base, group)].reshape(group * slots, qb))
        return dot(
            jnp.concatenate([sel, sel], axis=1), jnp.concatenate(parts, axis=0), 1, 0
        )

    g_sum = reduce_parts(gt, gsend, grx, gown, gxrx, gall, g_s, g_r)
    next(g_sum)
    next(g_sum)
    ebar[...] = add_group(0)
    next(g_sum)
    ebar[...] += add_group(1)
    next(g_sum)

    def add_later(p):
        ebar[...] += add_group(p)

    for p in range(2, min(nz, 4)):
        add_later(p)
    for p in range(4, nz):
        add_later(p)

    g = jnp.concatenate([gall[j] for j in range(4)], axis=1)
    ebh, ebl = split(ebar[...])
    coeff = dot3(split(g), (ebh, ebl), 1, 0)
    og = outs // nc
    for j in range(nc):
        csend[j] = coeff[j * og : (j + 1) * og]

    def c_copy(t):
        d = at(lax.div(t, 2), lax.rem(t, 2))
        return copy(csend.at[d], crx.at[c], c_s.at[t], c_r.at[c], b, d)

    @pl.loop(1, nc)
    def _(t):
        c_copy(nc - t).start()

    crx[c] = csend[c]

    @pl.loop(1, nc)
    def _(t):
        s = at(lax.div(t, 2), lax.rem(t, 2))
        copy(csend.at[0], crx.at[s], c_s.at[t], c_r.at[s], b, s).wait_recv()

    csum = crx[0]
    for j in range(1, nc):
        csum = csum + crx[j]
    csum = csum * scale[b]
    cown[...] = csum
    call[c] = csum

    def ca_copy(t):
        return copy(
            cown, call.at[c], ca_s.at[t], ca_r.at[c], b, at(lax.div(t, 2), lax.rem(t, 2))
        )

    @pl.loop(1, nc)
    def _(t):
        ca_copy(nc - t).start()

    @pl.loop(1, nc)
    def _(t):
        s = at(lax.div(t, 2), lax.rem(t, 2))
        copy(cown, call.at[s], ca_s.at[t], ca_r.at[s], b, s).wait_recv()

    scaled = jnp.concatenate([call[j] for j in range(nc)], axis=0)
    u = dot3(split(scaled), (ebh, ebl), 1, 1)
    u_sum = reduce_parts(u, usend, urx, uown, uxrx, uall, u_s, u_r)
    for _ in range(4):
        next(u_sum)
    for j in range(4):
        upd_v[:, j * piece : (j + 1) * piece] = uall[j] - gall[j]
    upd_store = pltpu.make_async_copy(upd_v, upd_out, out_s.at[1])
    upd_store.start()

    @pl.loop(1, nc)
    def _(t):
        f_copy(t).wait_send()
        p_copy(t).wait_send()
        r_copy(t).wait_send()
        c_copy(t).wait_send()
        ca_copy(t).wait_send()

    @pl.loop(0, n - 1)
    def _(t):
        e_copy(t).wait_send()
        o_copy(t).wait_send()

    next(g_sum)
    next(u_sum)
    res_store.wait()
    upd_store.wait()


def per_device(
    pool_features,
    pool_targets,
    batch_index,
    centers,
    weights,
    eig_vectors,
    eig_scale,
    nys_owner,
    nys_offset,
):
    nb, nc = lax.axis_size("batch"), lax.axis_size("centers")
    n = nb * nc
    rows, (pool, dim) = batch_index.shape[0], pool_features.shape
    outs = pool_targets.shape[1]
    cdev = centers.shape[0]
    pts, q = eig_vectors.shape
    slots = max(2, 2 * pts // nc)
    group, half = 2 * nb, nb // 2
    qb, piece, og = q // nb, cdev // 4, outs // nc
    vm = pltpu.VMEM
    dma = pltpu.SemaphoreType.DMA
    spec = pl.BlockSpec(memory_space=pl.ANY)
    pair = [dma((nc,)), dma((nc,))]
    every = [dma((n,)), dma((n,))]
    sums = [dma((half + 1,)), dma((half + 2,))]
    reduced = [
        vm((4, outs, piece), F32),
        vm((2, outs, piece), F32),
        vm((2, outs, piece), F32),
        vm((half, 2, outs, piece), F32),
        vm((4, outs, piece), F32),
    ]
    residual, update = pl.pallas_call(
        functools.partial(body, nb, nc),
        out_shape=(
            jax.ShapeDtypeStruct((rows, outs), F32),
            jax.ShapeDtypeStruct((outs, cdev), F32),
        ),
        in_specs=[spec] * 9,
        out_specs=(spec, spec),
        scratch_shapes=[
            vm((pool, dim), F32),
            vm((outs, pool), F32),
            vm((1, rows), jnp.int32),
            pltpu.SMEM((1, rows), jnp.int32),
            vm((cdev, dim), F32),
            vm((outs, cdev), F32),
            vm((pts, q), F32),
            vm((nb, 1, qb), F32),
            vm((1, pts), jnp.int32),
            vm((1, pts), jnp.int32),
            vm((rows, outs), F32),
            vm((outs, cdev), F32),
            vm((rows, dim), F32),
            vm((nc, rows, dim), F32),
            vm((cdev, 4 * dim), LOW),
            vm((2 * outs, cdev), LOW),
            vm((nc // 2, 2 * rows, cdev), LOW),
            vm((nc // 2, 2 * rows, cdev), LOW),
            vm((nc, rows // 2, 2 * outs), F32),
            vm((nc, rows // 2, 2 * outs), F32),
            vm((rows // 2, 2 * outs), F32),
            vm((nc, rows // 2, 2 * outs), F32),
            vm((nb, nc * slots, qb), F32),
            vm((n, slots, qb), F32),
            vm((nc, 1, group * slots), F32),
            vm((n, 1, group * slots), F32),
            vm((cdev, qb), F32),
        ]
        + reduced
        + [
            vm((nc, og, qb), F32),
            vm((nc, og, qb), F32),
            vm((og, qb), F32),
            vm((nc, og, qb), F32),
        ]
        + reduced
        + [dma((10,)), dma((2,))]
        + pair * 3
        + every * 2
        + sums
        + pair * 2
        + sums,
        compiler_params=pltpu.CompilerParams(collective_id=0, has_side_effects=True),
    )(
        pool_features,
        pool_targets.T,
        batch_index[None, :],
        centers,
        weights.T,
        eig_vectors,
        eig_scale.reshape(nb, 1, qb),
        nys_owner.reshape(1, pts),
        nys_offset[None, :],
    )
    return (residual, update.T)


def solution(mesh):
    placed = (
        P(("batch", "centers"), None),
        P(("batch", "centers"), None),
        P(("batch", "centers")),
        P("centers", None),
        P("centers", None),
        P(("batch", "centers"), None),
        P(),
        P(("batch", "centers"), None),
        P(("batch", "centers")),
    )
    return jax.shard_map(
        per_device,
        mesh=mesh,
        in_specs=placed,
        out_specs=(P(("batch", "centers"), None), P("centers", None)),
        check_vma=False,
    )
```

```python
import functools
import math

import jax
import jax.numpy as jnp
from jax import lax
from jax.experimental import pallas as pl
from jax.experimental.pallas import tpu as pltpu
from jax.sharding import PartitionSpec as P

DEPTH = 3
EPS = 1e-06
HIGH = lax.Precision.HIGHEST
VMEM = 32 * 2**20
MESH = pl.DeviceIdType.MESH
LOW = jnp.bfloat16
F32 = jnp.float32
FAR = (8, 0, 0, 0, 0, 16)
NEAR = (7, 0, 0, 0, 0, 16)
ACOS = (
    1.5707963050,
    -0.2145988016,
    0.0889789874,
    -0.0501743046,
    0.0308918810,
    -0.0170881256,
    0.0066700901,
    -0.0012624911,
)


def dot(a, b, ca, cb):
    return lax.dot_general(a, b, (((ca,), (cb,)), ((), ())), preferred_element_type=F32)


def exact(a, b, ca, cb):
    return lax.dot_general(
        a, b, (((ca,), (cb,)), ((), ())), precision=HIGH, preferred_element_type=F32
    )


def split(x):
    hi = x.astype(LOW)
    return hi, (x - hi.astype(F32)).astype(LOW)


def dot3(a, b, ca, cb):
    (ah, al), (bh, bl) = a, b
    rows = ah.shape[1 - ca]
    both = dot(jnp.concatenate([ah, al], axis=1 - ca), bh, ca, cb)
    return both[:rows] + both[rows:] + dot(ah, bl, ca, cb)


def fold(x):
    h = x.shape[0] // 2
    return jnp.concatenate([x[:h], x[h:]], axis=1)


def unfold(x):
    h = x.shape[1] // 2
    return jnp.concatenate([x[:, :h], x[:, h:]], axis=0)


def arc_parts(x):
    u = jnp.maximum(1.0 - x, 1e-30)
    poly = jnp.full_like(x, ACOS[-1] / math.pi)
    for a in ACOS[-2::-1]:
        poly = poly * x + a / math.pi
    v = u * (1.0 + x)
    return u * lax.rsqrt(u) * poly, v * lax.rsqrt(v) * (1.0 / math.pi)


def tangent_kernel(cosine):
    arc, sine = arc_parts(jnp.abs(cosine))
    remain = jnp.where(cosine < 0.0, arc, 1.0 - arc)
    prod = remain * cosine
    sigma = sine + prod
    tangent = sigma + prod
    for _ in range(DEPTH - 1):
        arc, sine = arc_parts(sigma)
        remain = 1.0 - arc
        sigma = sine + remain * sigma
        tangent = sigma + tangent * remain
    return tangent


def body(
    nb,
    nc,
    pool_f_h,
    pool_t_h,
    index_h,
    cen_h,
    wts_h,
    eig_h,
    scale_h,
    owner_h,
    offset_h,
    res_out,
    upd_out,
    pool_f,
    pool_t,
    index,
    index_s,
    cen,
    wts,
    eig,
    scale,
    owner,
    offset,
    res_v,
    upd_v,
    feat,
    feat_all,
    ccat,
    wcat,
    kh,
    kl,
    ppart,
    prx,
    rsend,
    rrx,
    packed,
    eigrx,
    offsend,
    offrx,
    ebar,
    gsend,
    grx,
    gown,
    gxrx,
    gall,
    csend,
    crx,
    cown,
    call,
    usend,
    urx,
    uown,
    uxrx,
    uall,
    in_s,
    out_s,
    told,
    f_s,
    f_r,
    p_s,
    p_r,
    r_s,
    r_r,
    e_s,
    e_r,
    o_s,
    o_r,
    g_s,
    g_r,
    c_s,
    c_r,
    ca_s,
    ca_r,
    u_s,
    u_r,
):
    b = lax.axis_index("batch")
    c = lax.axis_index("centers")
    n = nb * nc
    me = b * nc + c
    half = nb // 2
    k2, x = lax.rem(b, 2), lax.div(b, 2)
    z, y = lax.div(c, 2), lax.rem(c, 2)
    nz = nc // 2
    mine = c * nb + b
    rows, dim = feat.shape
    outs, cdev = wts.shape
    pts = owner.shape[1]
    group = 2 * nb
    slots = packed.shape[1] // nc
    qb = packed.shape[2]
    piece = cdev // 4
    rows_total = rows * n

    def copy(src, dst, ssem, rsem, db, dc):
        return pltpu.make_async_remote_copy(
            src_ref=src,
            dst_ref=dst,
            send_sem=ssem,
            recv_sem=rsem,
            device_id=(db, dc),
            device_id_type=MESH,
        )

    barrier = pltpu.get_barrier_semaphore()

    def greet(zd, first):
        @pl.loop(first, group)
        def _(i):
            o = lax.rem(b + (y * nb) + i, group)
            pl.semaphore_signal(
                barrier,
                inc=1,
                device_id=(lax.rem(o, nb), zd * 2 + lax.div(o, nb)),
                device_id_type=MESH,
            )

    greet(z, 1)

    @pl.when(z > 0)
    def _():
        greet(z - 1, 0)

    @pl.when(z < nz - 1)
    def _():
        greet(z + 1, 0)

    loads = [
        pltpu.make_async_copy(src, dst, in_s.at[i])
        for i, (src, dst) in enumerate(
            (
                (index_h, index_s),
                (pool_f_h, pool_f),
                (owner_h, owner),
                (offset_h, offset),
                (eig_h, eig),
                (cen_h, cen),
                (wts_h, wts),
                (scale_h, scale),
                (index_h, index),
                (pool_t_h, pool_t),
            )
        )
    ]
    for load in loads:
        load.start()

    loads[0].wait()
    loads[1].wait()

    @pl.loop(0, rows, unroll=8)
    def _(j):
        feat[pl.ds(j, 1), :] = pool_f[pl.ds(index_s[0, j], 1), :]

    feat_all[c] = feat[...]

    inner = jnp.logical_and(z > 0, z < nz - 1)

    @pl.when(inner)
    def _():
        pl.semaphore_wait(barrier, 3 * group - 1)

    @pl.when(jnp.logical_not(inner))
    def _():
        pl.semaphore_wait(barrier, 2 * group - 1)

    def at(zo, yo):
        return (z ^ zo) * 2 + (y ^ yo)

    mate = at(0, 1)

    def spread(src, dst, ssem, rsem, t):
        p, on = lax.div(t, 2), lax.rem(t, 2)
        s = at(p * on, 0)
        d = at(p * (1 - on), on)
        return copy(src if src is not None else dst.at[s], dst.at[s], ssem.at[t], rsem.at[s], b, d)

    def spread_pass(dst, ssem, rsem, p):
        s = at(p, 0)
        copy(dst.at[s], dst.at[s], ssem.at[0], rsem.at[s], b, s).wait_recv()
        spread(None, dst, ssem, rsem, 2 * p + 1).start()

    def spread_end(dst, ssem, rsem, p):
        s = at(p, 1)
        copy(dst.at[s], dst.at[s], ssem.at[0], rsem.at[s], b, s).wait_recv()

    def spread_sent(src, dst, ssem, rsem):
        spread(src, dst, ssem, rsem, 1).wait_send()

        @pl.loop(2, nc)
        def _(t):
            spread(None, dst, ssem, rsem, t).wait_send()

    def tell(which, zd):
        pl.semaphore_signal(
            told.at[which], inc=1, device_id=(b, zd * 2 + y), device_id_type=MESH
        )

    @pl.when(z == 1)
    def _():
        tell(0, z + 1)

    @pl.when(z == nz - 2)
    def _():
        tell(1, z - 1)

    @pl.loop(1, nz)
    def _(p):
        @pl.when(jnp.abs((z ^ p) - z) == 1)
        def _():
            spread(feat, feat_all, f_s, f_r, 2 * p).start()

    spread(feat, feat_all, f_s, f_r, 1).start()

    def hear():
        @pl.when(z >= 2)
        def _():
            pl.semaphore_wait(told.at[0], 1)

            @pl.when(z < nz - 1)
            def _():
                tell(0, z + 1)

        @pl.when(z <= nz - 3)
        def _():
            pl.semaphore_wait(told.at[1], 1)

            @pl.when(z > 0)
            def _():
                tell(1, z - 1)

        @pl.loop(1, nz)
        def _(i):
            p = nz - i

            @pl.when(jnp.abs((z ^ p) - z) > 1)
            def _():
                spread(feat, feat_all, f_s, f_r, 2 * p).start()

    @pl.when(z >= nz // 2)
    def _():
        hear()

    loads[2].wait()
    loads[3].wait()
    own = owner[...]
    hot = (own == lax.broadcasted_iota(jnp.int32, (nc, pts), 0)).astype(F32)
    upper = (
        lax.broadcasted_iota(jnp.int32, (pts, pts), 0)
        < lax.broadcasted_iota(jnp.int32, (pts, pts), 1)
    ).astype(F32)
    rank = jnp.sum(
        dot(hot.astype(LOW), upper.astype(LOW), 1, 0) * hot, axis=0, keepdims=True
    ).astype(jnp.int32)
    place = (
        (lax.broadcasted_iota(jnp.int32, (nc * slots, pts), 0) == own * slots + rank)
        .astype(F32)
        .astype(LOW)
    )
    loads[4].wait()
    both = jnp.concatenate(split(eig[...]), axis=0)
    place2 = jnp.concatenate([place, place], axis=1)
    for j in range(nb):
        packed[j] = dot(place2, both[:, j * qb : (j + 1) * qb], 1, 0)
    here = (
        lax.broadcasted_iota(jnp.int32, (group * slots, pts), 0)
        == (y * nb + b) * slots + rank
    ).astype(F32)
    marks = exact(hot * (offset[...].astype(F32) + 1.0), here, 1, 1)
    for j in range(nc):
        offsend[j] = marks[j : j + 1]
    eigrx[mine] = packed[b, pl.ds(pl.multiple_of(c * slots, slots), slots)]
    offrx[mine] = offsend[c]

    loads[5].wait()
    cval = cen[...]
    csq = cval * cval
    ncol = jnp.mean(csq, axis=1, keepdims=True) + EPS
    ch, cl = split(cval / (jnp.sqrt(ncol) * dim))
    ccat[...] = jnp.concatenate([ch, cl, ch, cl], axis=1)
    sb_row = jnp.sqrt(exact(jnp.full((8, dim), 1.0 / dim, F32), csq, 1, 1)[0:1] + EPS)
    loads[6].wait()
    wcat[...] = jnp.concatenate(split(wts[...] * sb_row), axis=0)

    @pl.when(z < nz // 2)
    def _():
        hear()

    def e_place(t):
        o = n - 1 - t
        return lax.rem(b + lax.rem(o, nb), nb), at(lax.div(o, group), lax.rem(lax.div(o, nb), 2))

    def e_source(o):
        return lax.rem(b - lax.rem(o, nb) + nb, nb), at(
            lax.div(o, group), lax.rem(lax.div(o, nb), 2)
        )

    def e_copy(t):
        db, dc = e_place(t)
        return copy(
            packed.at[db, pl.ds(pl.multiple_of(dc * slots, slots), slots)],
            eigrx.at[mine],
            e_s.at[t],
            e_r.at[mine],
            db,
            dc,
        )

    def o_copy(t):
        db, dc = e_place(t)
        return copy(offsend.at[dc], offrx.at[mine], o_s.at[t], o_r.at[mine], db, dc)

    marks_at = [0, n // 2]
    ends_at = [n // 2, n - 1]

    def e_start(step):
        for kind, plan in enumerate((FAR, NEAR)):
            lo, total = marks_at[kind], ends_at[kind]
            hi = total if step == len(plan) - 1 else min(total, lo + plan[step] * n // 32)
            marks_at[kind] = hi

            @pl.loop(lo, hi)
            def _(t):
                e_copy(t).start()

    e_start(0)

    def p_copy(t):
        s = at(lax.div(t, 2), lax.rem(t, 2))
        return copy(ppart.at[s], prx.at[c], p_s.at[t], p_r.at[c], b, s)

    def pair(p):
        zs = z ^ p
        av = feat_all[pl.ds(zs * 2, 2)].reshape(2 * rows, dim)
        na = jnp.mean(av * av, axis=1, keepdims=True) + EPS
        ah, al = split(av * lax.rsqrt(na))
        k = tangent_kernel(dot(jnp.concatenate([ah, ah, al, al], axis=1), ccat[...], 1, 1))
        hi, lo = split(k)
        kh[zs] = hi
        kl[zs] = lo
        top = dot(hi, wcat[...], 1, 1)
        pred = top[:, :outs] + top[:, outs:] + dot(lo, wcat[:outs], 1, 1)
        return fold(pred[:rows]), fold(pred[rows:])

    spread_end(feat_all, f_s, f_r, 0)
    low, high = pair(0)
    prx[c] = jnp.where(y == 0, low, high)
    ppart[c ^ 1] = jnp.where(y == 0, high, low)
    p_copy(1).start()
    e_start(1)

    def later(p):
        spread_end(feat_all, f_s, f_r, p)
        lo, hi = pair(p)
        zs = (z ^ p) * 2
        ppart[zs] = lo
        ppart[zs + 1] = hi
        p_copy(2 * p).start()
        p_copy(2 * p + 1).start()

    spread_pass(feat_all, f_s, f_r, 1)
    spread_pass(feat_all, f_s, f_r, 2)
    later(1)
    e_start(2)
    spread_pass(feat_all, f_s, f_r, 3)
    later(2)
    e_start(3)

    @pl.loop(3, nz - 1)
    def _(p):
        spread_pass(feat_all, f_s, f_r, p + 1)
        later(p)

    later(nz - 1)
    e_start(4)

    a = feat[...]
    sa = jnp.sqrt(jnp.mean(a * a, axis=1, keepdims=True) + EPS)
    loads[7].wait()
    loads[8].wait()
    loads[9].wait()
    drawn = (
        (lax.broadcasted_iota(jnp.int32, (pool_t.shape[1], rows), 0) == index[...])
        .astype(F32)
        .astype(LOW)
    )
    th, tl = split(pool_t[...])
    picked = dot(jnp.concatenate([th, tl], axis=0), drawn, 1, 0)
    targ = (picked[:outs] + picked[outs:]).T

    @pl.loop(1, nc)
    def _(t):
        s = at(lax.div(t, 2), lax.rem(t, 2))
        copy(ppart.at[s], prx.at[s], p_s.at[t], p_r.at[s], b, s).wait_recv()

    pred = prx[0]
    for j in range(1, nc):
        pred = pred + prx[j]
    resid = unfold(pred) * sa - targ
    folded = fold(resid * (sa / math.sqrt(rows_total)))
    rsend[...] = folded
    rrx[c] = folded

    def r_copy(t):
        return copy(
            rsend, rrx.at[c], r_s.at[t], r_r.at[c], b, at(lax.div(t, 2), lax.rem(t, 2))
        )

    @pl.loop(1, nc)
    def _(t):
        r_copy(nc - t).start()

    @pl.loop(0, n - 1)
    def _(t):
        o_copy(t).start()

    e_start(5)

    res_v[...] = resid
    res_store = pltpu.make_async_copy(res_v, res_out, out_s.at[0])
    res_store.start()

    @pl.loop(1, nc)
    def _(t):
        s = at(lax.div(t, 2), lax.rem(t, 2))
        copy(rsend, rrx.at[s], r_s.at[t], r_r.at[s], b, s).wait_recv()

    every = jnp.concatenate([unfold(rrx[j]) for j in range(nc)], axis=0)
    eh, el = split(every)
    khv = kh[...].reshape(nc * rows, cdev)
    up = dot(jnp.concatenate([eh, el], axis=1), khv, 0, 0)
    gt = (
        up[:outs] + up[outs:] + dot(eh, kl[...].reshape(nc * rows, cdev), 0, 0)
    ) * sb_row

    def reduce_parts(part, send, rx, owned, xrx, full, ssem, rsem):
        mate = b + 1 - 2 * k2
        started = []
        for j in range(4):
            send[j] = part[:, j * piece : (j + 1) * piece]
        away = copy(
            send.at[pl.ds(2 * (1 - k2), 2)], rx, ssem.at[0], rsem.at[0], mate, c
        )
        away.start()
        started.append(away)
        yield
        away.wait_recv()
        owned[...] = send[pl.ds(2 * k2, 2)] + rx[...]
        for i in range(1, half):
            d = lax.rem(x + i, half) * 2 + k2
            out = copy(owned, xrx.at[x], ssem.at[i], rsem.at[1 + x], d, c)
            out.start()
            started.append(out)
        yield
        total = owned[...]
        for i in range(1, half):
            s = lax.rem(x + i, half)
            copy(owned, xrx.at[s], ssem.at[i], rsem.at[1 + s], s * 2 + k2, c).wait_recv()
            total = total + xrx[s]
        full[pl.ds(2 * k2, 2)] = total
        across = copy(
            full.at[pl.ds(2 * k2, 2)],
            full.at[pl.ds(2 * k2, 2)],
            ssem.at[half],
            rsem.at[1 + half],
            mate,
            c,
        )
        across.start()
        started.append(across)
        yield
        copy(
            full.at[pl.ds(2 * k2, 2)],
            full.at[pl.ds(2 * (1 - k2), 2)],
            ssem.at[half],
            rsem.at[1 + half],
            mate,
            c,
        ).wait_recv()
        yield
        for s in started:
            s.wait_send()
        yield

    def add_group(p):
        zs = z ^ p
        base = zs * group

        @pl.loop(1 if p == 0 else 0, group)
        def _(i):
            sb, sc = e_source(p * group + i)
            s = sc * nb + sb
            t = n - 1 - (p * group + i)
            copy(offsend.at[0], offrx.at[s], o_s.at[t], o_r.at[s], b, c).wait_recv()
            copy(packed.at[0, pl.ds(0, slots)], eigrx.at[s], e_s.at[t], e_r.at[s], b, c).wait_recv()

        mark = offrx[base]
        for i in range(1, group):
            mark = mark + offrx[base + i]
        sel = (
            (
                lax.broadcasted_iota(jnp.int32, (cdev, group * slots), 0) + 1
                == mark.astype(jnp.int32)
            )
            .astype(F32)
            .astype(LOW)
        )
        parts = split(eigrx[pl.ds(base, group)].reshape(group * slots, qb))
        return dot(
            jnp.concatenate([sel, sel], axis=1), jnp.concatenate(parts, axis=0), 1, 0
        )

    g_sum = reduce_parts(gt, gsend, grx, gown, gxrx, gall, g_s, g_r)
    next(g_sum)
    next(g_sum)
    ebar[...] = add_group(0)
    next(g_sum)
    ebar[...] += add_group(1)
    next(g_sum)

    def add_later(p):
        ebar[...] += add_group(p)

    for p in range(2, min(nz, 4)):
        add_later(p)
    for p in range(4, nz):
        add_later(p)

    g = jnp.concatenate([gall[j] for j in range(4)], axis=1)
    ebh, ebl = split(ebar[...])
    coeff = dot3(split(g), (ebh, ebl), 1, 0)
    og = outs // nc
    for j in range(nc):
        csend[j] = coeff[j * og : (j + 1) * og]

    def c_copy(t):
        d = at(lax.div(t, 2), lax.rem(t, 2))
        return copy(csend.at[d], crx.at[c], c_s.at[t], c_r.at[c], b, d)

    @pl.loop(1, nc)
    def _(t):
        c_copy(nc - t).start()

    crx[c] = csend[c]

    @pl.loop(1, nc)
    def _(t):
        s = at(lax.div(t, 2), lax.rem(t, 2))
        copy(csend.at[0], crx.at[s], c_s.at[t], c_r.at[s], b, s).wait_recv()

    csum = crx[0]
    for j in range(1, nc):
        csum = csum + crx[j]
    csum = csum * scale[b]
    cown[...] = csum
    call[c] = csum

    def ca_copy(t):
        return copy(
            cown, call.at[c], ca_s.at[t], ca_r.at[c], b, at(lax.div(t, 2), lax.rem(t, 2))
        )

    @pl.loop(1, nc)
    def _(t):
        ca_copy(nc - t).start()

    @pl.loop(1, nc)
    def _(t):
        s = at(lax.div(t, 2), lax.rem(t, 2))
        copy(cown, call.at[s], ca_s.at[t], ca_r.at[s], b, s).wait_recv()

    scaled = jnp.concatenate([call[j] for j in range(nc)], axis=0)
    u = dot3(split(scaled), (ebh, ebl), 1, 1)
    u_sum = reduce_parts(u, usend, urx, uown, uxrx, uall, u_s, u_r)
    for _ in range(4):
        next(u_sum)
    for j in range(4):
        upd_v[:, j * piece : (j + 1) * piece] = uall[j] - gall[j]
    upd_store = pltpu.make_async_copy(upd_v, upd_out, out_s.at[1])
    upd_store.start()

    spread_sent(feat, feat_all, f_s, f_r)

    @pl.loop(1, nc)
    def _(t):
        p_copy(t).wait_send()
        r_copy(t).wait_send()
        c_copy(t).wait_send()
        ca_copy(t).wait_send()

    @pl.loop(0, n - 1)
    def _(t):
        e_copy(t).wait_send()
        o_copy(t).wait_send()

    next(g_sum)
    next(u_sum)
    res_store.wait()
    upd_store.wait()


def per_device(
    pool_features,
    pool_targets,
    batch_index,
    centers,
    weights,
    eig_vectors,
    eig_scale,
    nys_owner,
    nys_offset,
):
    nb, nc = lax.axis_size("batch"), lax.axis_size("centers")
    n = nb * nc
    rows, (pool, dim) = batch_index.shape[0], pool_features.shape
    outs = pool_targets.shape[1]
    cdev = centers.shape[0]
    pts, q = eig_vectors.shape
    slots = max(2, 2 * pts // nc)
    group, half = 2 * nb, nb // 2
    qb, piece, og = q // nb, cdev // 4, outs // nc
    vm = pltpu.VMEM
    dma = pltpu.SemaphoreType.DMA
    spec = pl.BlockSpec(memory_space=pl.ANY)
    pair = [dma((nc,)), dma((nc,))]
    every = [dma((n,)), dma((n,))]
    sums = [dma((half + 1,)), dma((half + 2,))]
    reduced = [
        vm((4, outs, piece), F32),
        vm((2, outs, piece), F32),
        vm((2, outs, piece), F32),
        vm((half, 2, outs, piece), F32),
        vm((4, outs, piece), F32),
    ]
    residual, update = pl.pallas_call(
        functools.partial(body, nb, nc),
        out_shape=(
            jax.ShapeDtypeStruct((rows, outs), F32),
            jax.ShapeDtypeStruct((outs, cdev), F32),
        ),
        in_specs=[pl.BlockSpec(memory_space=pltpu.HBM)] * 9,
        out_specs=(spec, spec),
        scratch_shapes=[
            vm((pool, dim), F32),
            vm((outs, pool), F32),
            vm((1, rows), jnp.int32),
            pltpu.SMEM((1, rows), jnp.int32),
            vm((cdev, dim), F32),
            vm((outs, cdev), F32),
            vm((pts, q), F32),
            vm((nb, 1, qb), F32),
            vm((1, pts), jnp.int32),
            vm((1, pts), jnp.int32),
            vm((rows, outs), F32),
            vm((outs, cdev), F32),
            vm((rows, dim), F32),
            vm((nc, rows, dim), F32),
            vm((cdev, 4 * dim), LOW),
            vm((2 * outs, cdev), LOW),
            vm((nc // 2, 2 * rows, cdev), LOW),
            vm((nc // 2, 2 * rows, cdev), LOW),
            vm((nc, rows // 2, 2 * outs), F32),
            vm((nc, rows // 2, 2 * outs), F32),
            vm((rows // 2, 2 * outs), F32),
            vm((nc, rows // 2, 2 * outs), F32),
            vm((nb, nc * slots, qb), F32),
            vm((n, slots, qb), F32),
            vm((nc, 1, group * slots), F32),
            vm((n, 1, group * slots), F32),
            vm((cdev, qb), F32),
        ]
        + reduced
        + [
            vm((nc, og, qb), F32),
            vm((nc, og, qb), F32),
            vm((og, qb), F32),
            vm((nc, og, qb), F32),
        ]
        + reduced
        + [dma((10,)), dma((2,)), pltpu.SemaphoreType.REGULAR((2,))]
        + pair * 3
        + every * 2
        + sums
        + pair * 2
        + sums,
        compiler_params=pltpu.CompilerParams(
            collective_id=0, has_side_effects=True, vmem_limit_bytes=VMEM
        ),
    )(
        *(
            pltpu.with_memory_space_constraint(array, pltpu.HBM)
            for array in (
                pool_features,
                pool_targets.T,
                batch_index[None, :],
                centers,
                weights.T,
                eig_vectors,
                eig_scale.reshape(nb, 1, qb),
                nys_owner.reshape(1, pts),
                nys_offset[None, :],
            )
        )
    )
    return (residual, update.T)


def solution(mesh):
    placed = (
        P(("batch", "centers"), None),
        P(("batch", "centers"), None),
        P(("batch", "centers")),
        P("centers", None),
        P("centers", None),
        P(("batch", "centers"), None),
        P(),
        P(("batch", "centers"), None),
        P(("batch", "centers")),
    )
    return jax.shard_map(
        per_device,
        mesh=mesh,
        in_specs=placed,
        out_specs=(P(("batch", "centers"), None), P("centers", None)),
        check_vma=False,
    )
```

```python
import functools
import math

import jax
import jax.numpy as jnp
from jax import lax
from jax.experimental import pallas as pl
from jax.experimental.pallas import tpu as pltpu
from jax.sharding import PartitionSpec as P

DEPTH = 3
EPS = 1e-06
HIGH = lax.Precision.HIGHEST
VMEM = 32 * 2**20
MESH = pl.DeviceIdType.MESH
LOW = jnp.bfloat16
F32 = jnp.float32
FAR = (8, 0, 0, 0, 0, 16)
NEAR = (7, 0, 0, 0, 0, 16)
ACOS = (
    1.5707963050,
    -0.2145988016,
    0.0889789874,
    -0.0501743046,
    0.0308918810,
    -0.0170881256,
    0.0066700901,
    -0.0012624911,
)


def dot(a, b, ca, cb):
    return lax.dot_general(a, b, (((ca,), (cb,)), ((), ())), preferred_element_type=F32)


def exact(a, b, ca, cb):
    return lax.dot_general(
        a, b, (((ca,), (cb,)), ((), ())), precision=HIGH, preferred_element_type=F32
    )


def split(x):
    hi = x.astype(LOW)
    return hi, (x - hi.astype(F32)).astype(LOW)


def dot3(a, b, ca, cb):
    (ah, al), (bh, bl) = a, b
    rows = ah.shape[1 - ca]
    both = dot(jnp.concatenate([ah, al], axis=1 - ca), bh, ca, cb)
    return both[:rows] + both[rows:] + dot(ah, bl, ca, cb)


def fold(x):
    h = x.shape[0] // 2
    return jnp.concatenate([x[:h], x[h:]], axis=1)


def unfold(x):
    h = x.shape[1] // 2
    return jnp.concatenate([x[:, :h], x[:, h:]], axis=0)


def arc_parts(x):
    u = jnp.maximum(1.0 - x, 1e-30)
    poly = jnp.full_like(x, ACOS[-1] / math.pi)
    for a in ACOS[-2::-1]:
        poly = poly * x + a / math.pi
    v = u * (1.0 + x)
    return u * lax.rsqrt(u) * poly, v * lax.rsqrt(v) * (1.0 / math.pi)


def tangent_kernel(cosine):
    arc, sine = arc_parts(jnp.abs(cosine))
    remain = jnp.where(cosine < 0.0, arc, 1.0 - arc)
    prod = remain * cosine
    sigma = sine + prod
    tangent = sigma + prod
    for _ in range(DEPTH - 1):
        arc, sine = arc_parts(sigma)
        remain = 1.0 - arc
        sigma = sine + remain * sigma
        tangent = sigma + tangent * remain
    return tangent


def body(
    nb,
    nc,
    pool_f_h,
    pool_t_h,
    index_h,
    cen_h,
    wts_h,
    eig_h,
    scale_h,
    owner_h,
    offset_h,
    res_out,
    upd_out,
    pool_f,
    pool_t,
    index,
    index_s,
    cen,
    wts,
    eig,
    scale,
    owner,
    offset,
    res_v,
    upd_v,
    feat,
    feat_all,
    ccat,
    wcat,
    kh,
    kl,
    ppart,
    prx,
    rsend,
    rrx,
    packed,
    eigrx,
    offsend,
    offrx,
    ebar,
    gsend,
    grx,
    gown,
    gxrx,
    gall,
    csend,
    crx,
    cown,
    call,
    usend,
    urx,
    uown,
    uxrx,
    uall,
    in_s,
    out_s,
    told,
    f_s,
    f_r,
    p_s,
    p_r,
    r_s,
    r_r,
    e_s,
    e_r,
    o_s,
    o_r,
    g_s,
    g_r,
    c_s,
    c_r,
    ca_s,
    ca_r,
    u_s,
    u_r,
):
    b = lax.axis_index("batch")
    c = lax.axis_index("centers")
    n = nb * nc
    me = b * nc + c
    half = nb // 2
    k2, x = lax.rem(b, 2), lax.div(b, 2)
    z, y = lax.div(c, 2), lax.rem(c, 2)
    nz = nc // 2
    mine = c * nb + b
    rows, dim = feat.shape
    outs, cdev = wts.shape
    pts = owner.shape[1]
    group = 2 * nb
    slots = packed.shape[1] // nc
    qb = packed.shape[2]
    piece = cdev // 4
    rows_total = rows * n

    def copy(src, dst, ssem, rsem, db, dc):
        return pltpu.make_async_remote_copy(
            src_ref=src,
            dst_ref=dst,
            send_sem=ssem,
            recv_sem=rsem,
            device_id=(db, dc),
            device_id_type=MESH,
        )

    barrier = pltpu.get_barrier_semaphore()

    def greet(zd, first):
        @pl.loop(first, group)
        def _(i):
            o = lax.rem(b + (y * nb) + i, group)
            pl.semaphore_signal(
                barrier,
                inc=1,
                device_id=(lax.rem(o, nb), zd * 2 + lax.div(o, nb)),
                device_id_type=MESH,
            )

    greet(z, 1)

    @pl.when(z > 0)
    def _():
        greet(z - 1, 0)

    @pl.when(z < nz - 1)
    def _():
        greet(z + 1, 0)

    loads = [
        pltpu.make_async_copy(src, dst, in_s.at[i])
        for i, (src, dst) in enumerate(
            (
                (index_h, index_s),
                (pool_f_h, pool_f),
                (owner_h, owner),
                (offset_h, offset),
                (eig_h, eig),
                (cen_h, cen),
                (wts_h, wts),
                (scale_h, scale),
                (index_h, index),
                (pool_t_h, pool_t),
            )
        )
    ]
    for load in loads:
        load.start()

    loads[0].wait()
    loads[1].wait()

    @pl.loop(0, rows, unroll=8)
    def _(j):
        feat[pl.ds(j, 1), :] = pool_f[pl.ds(index_s[0, j], 1), :]

    feat_all[c] = feat[...]

    inner = jnp.logical_and(z > 0, z < nz - 1)

    @pl.when(inner)
    def _():
        pl.semaphore_wait(barrier, 3 * group - 1)

    @pl.when(jnp.logical_not(inner))
    def _():
        pl.semaphore_wait(barrier, 2 * group - 1)

    def at(zo, yo):
        return (z ^ zo) * 2 + (y ^ yo)

    mate = at(0, 1)

    def spread(src, dst, ssem, rsem, t):
        p, on = lax.div(t, 2), lax.rem(t, 2)
        s = at(p * on, 0)
        d = at(p * (1 - on), on)
        return copy(src if src is not None else dst.at[s], dst.at[s], ssem.at[t], rsem.at[s], b, d)

    def spread_pass(dst, ssem, rsem, p):
        s = at(p, 0)
        copy(dst.at[s], dst.at[s], ssem.at[0], rsem.at[s], b, s).wait_recv()
        spread(None, dst, ssem, rsem, 2 * p + 1).start()

    def spread_end(dst, ssem, rsem, p):
        s = at(p, 1)
        copy(dst.at[s], dst.at[s], ssem.at[0], rsem.at[s], b, s).wait_recv()

    def spread_sent(src, dst, ssem, rsem):
        spread(src, dst, ssem, rsem, 1).wait_send()

        @pl.loop(2, nc)
        def _(t):
            spread(None, dst, ssem, rsem, t).wait_send()

    def tell(which, zd):
        pl.semaphore_signal(
            told.at[which], inc=1, device_id=(b, zd * 2 + y), device_id_type=MESH
        )

    @pl.when(z == 1)
    def _():
        tell(0, z + 1)

    @pl.when(z == nz - 2)
    def _():
        tell(1, z - 1)

    @pl.loop(1, nz)
    def _(p):
        @pl.when(jnp.abs((z ^ p) - z) == 1)
        def _():
            spread(feat, feat_all, f_s, f_r, 2 * p).start()

    spread(feat, feat_all, f_s, f_r, 1).start()

    def hear():
        @pl.when(z >= 2)
        def _():
            pl.semaphore_wait(told.at[0], 1)

            @pl.when(z < nz - 1)
            def _():
                tell(0, z + 1)

        @pl.when(z <= nz - 3)
        def _():
            pl.semaphore_wait(told.at[1], 1)

            @pl.when(z > 0)
            def _():
                tell(1, z - 1)

        @pl.loop(1, nz)
        def _(i):
            p = nz - i

            @pl.when(jnp.abs((z ^ p) - z) > 1)
            def _():
                spread(feat, feat_all, f_s, f_r, 2 * p).start()

    @pl.when(z >= nz // 2)
    def _():
        hear()

    loads[2].wait()
    loads[3].wait()
    own = owner[...]
    hot = (own == lax.broadcasted_iota(jnp.int32, (nc, pts), 0)).astype(F32)
    upper = (
        lax.broadcasted_iota(jnp.int32, (pts, pts), 0)
        < lax.broadcasted_iota(jnp.int32, (pts, pts), 1)
    ).astype(F32)
    rank = jnp.sum(
        dot(hot.astype(LOW), upper.astype(LOW), 1, 0) * hot, axis=0, keepdims=True
    ).astype(jnp.int32)
    place = (
        (lax.broadcasted_iota(jnp.int32, (nc * slots, pts), 0) == own * slots + rank)
        .astype(F32)
        .astype(LOW)
    )
    loads[4].wait()
    both = jnp.concatenate(split(eig[...]), axis=0)
    place2 = jnp.concatenate([place, place], axis=1)
    for j in range(nb):
        packed[j] = dot(place2, both[:, j * qb : (j + 1) * qb], 1, 0)
    here = (
        lax.broadcasted_iota(jnp.int32, (group * slots, pts), 0)
        == (y * nb + b) * slots + rank
    ).astype(F32)
    marks = exact(hot * (offset[...].astype(F32) + 1.0), here, 1, 1)
    for j in range(nc):
        offsend[j] = marks[j : j + 1]
    eigrx[mine] = packed[b, pl.ds(pl.multiple_of(c * slots, slots), slots)]
    offrx[mine] = offsend[c]

    loads[5].wait()
    cval = cen[...]
    csq = cval * cval
    ncol = jnp.mean(csq, axis=1, keepdims=True) + EPS
    ch, cl = split(cval / (jnp.sqrt(ncol) * dim))
    ccat[...] = jnp.concatenate([ch, cl, ch, cl], axis=1)
    sb_row = jnp.sqrt(exact(jnp.full((8, dim), 1.0 / dim, F32), csq, 1, 1)[0:1] + EPS)
    loads[6].wait()
    wcat[...] = jnp.concatenate(split(wts[...] * sb_row), axis=0)

    @pl.when(z < nz // 2)
    def _():
        hear()

    def e_place(t):
        o = jnp.where(t < n // 2, n - 1 - t, t - n // 2 + 1)
        return lax.rem(b + lax.rem(o, nb), nb), at(lax.div(o, group), lax.rem(lax.div(o, nb), 2))

    def e_source(o):
        return lax.rem(b - lax.rem(o, nb) + nb, nb), at(
            lax.div(o, group), lax.rem(lax.div(o, nb), 2)
        )

    def e_copy(t):
        db, dc = e_place(t)
        return copy(
            packed.at[db, pl.ds(pl.multiple_of(dc * slots, slots), slots)],
            eigrx.at[mine],
            e_s.at[t],
            e_r.at[mine],
            db,
            dc,
        )

    def o_copy(t):
        db, dc = e_place(t)
        return copy(offsend.at[dc], offrx.at[mine], o_s.at[t], o_r.at[mine], db, dc)

    marks_at = [0, n // 2]
    ends_at = [n // 2, n - 1]

    def e_start(step):
        for kind, plan in enumerate((FAR, NEAR)):
            lo, total = marks_at[kind], ends_at[kind]
            hi = total if step == len(plan) - 1 else min(total, lo + plan[step] * n // 32)
            marks_at[kind] = hi

            @pl.loop(lo, hi)
            def _(t):
                e_copy(t).start()

    e_start(0)

    def p_copy(t):
        s = at(lax.div(t, 2), lax.rem(t, 2))
        return copy(ppart.at[s], prx.at[c], p_s.at[t], p_r.at[c], b, s)

    def pair(p):
        zs = z ^ p
        av = feat_all[pl.ds(zs * 2, 2)].reshape(2 * rows, dim)
        na = jnp.mean(av * av, axis=1, keepdims=True) + EPS
        ah, al = split(av * lax.rsqrt(na))
        k = tangent_kernel(dot(jnp.concatenate([ah, ah, al, al], axis=1), ccat[...], 1, 1))
        hi, lo = split(k)
        kh[zs] = hi
        kl[zs] = lo
        top = dot(hi, wcat[...], 1, 1)
        pred = top[:, :outs] + top[:, outs:] + dot(lo, wcat[:outs], 1, 1)
        return fold(pred[:rows]), fold(pred[rows:])

    spread_end(feat_all, f_s, f_r, 0)
    low, high = pair(0)
    prx[c] = jnp.where(y == 0, low, high)
    ppart[c ^ 1] = jnp.where(y == 0, high, low)
    p_copy(1).start()
    e_start(1)

    def later(p):
        spread_end(feat_all, f_s, f_r, p)
        lo, hi = pair(p)
        zs = (z ^ p) * 2
        ppart[zs] = lo
        ppart[zs + 1] = hi
        p_copy(2 * p).start()
        p_copy(2 * p + 1).start()

    spread_pass(feat_all, f_s, f_r, 1)
    spread_pass(feat_all, f_s, f_r, 2)
    later(1)
    e_start(2)
    spread_pass(feat_all, f_s, f_r, 3)
    later(2)
    e_start(3)

    @pl.loop(3, nz - 1)
    def _(p):
        spread_pass(feat_all, f_s, f_r, p + 1)
        later(p)

    later(nz - 1)
    e_start(4)

    @pl.loop(0, n - 1)
    def _(t):
        o_copy(t).start()

    a = feat[...]
    sa = jnp.sqrt(jnp.mean(a * a, axis=1, keepdims=True) + EPS)
    loads[7].wait()
    loads[8].wait()
    loads[9].wait()
    drawn = (
        (lax.broadcasted_iota(jnp.int32, (pool_t.shape[1], rows), 0) == index[...])
        .astype(F32)
        .astype(LOW)
    )
    th, tl = split(pool_t[...])
    picked = dot(jnp.concatenate([th, tl], axis=0), drawn, 1, 0)
    targ = (picked[:outs] + picked[outs:]).T

    @pl.loop(1, nc)
    def _(t):
        s = at(lax.div(t, 2), lax.rem(t, 2))
        copy(ppart.at[s], prx.at[s], p_s.at[t], p_r.at[s], b, s).wait_recv()

    pred = prx[0]
    for j in range(1, nc):
        pred = pred + prx[j]
    resid = unfold(pred) * sa - targ
    folded = fold(resid * (sa / math.sqrt(rows_total)))
    rsend[...] = folded
    rrx[c] = folded

    def r_copy(t):
        return copy(
            rsend, rrx.at[c], r_s.at[t], r_r.at[c], b, at(lax.div(t, 2), lax.rem(t, 2))
        )

    @pl.loop(1, nc)
    def _(t):
        r_copy(nc - t).start()

    e_start(5)

    res_v[...] = resid
    res_store = pltpu.make_async_copy(res_v, res_out, out_s.at[0])
    res_store.start()

    @pl.loop(1, nc)
    def _(t):
        s = at(lax.div(t, 2), lax.rem(t, 2))
        copy(rsend, rrx.at[s], r_s.at[t], r_r.at[s], b, s).wait_recv()

    every = jnp.concatenate([unfold(rrx[j]) for j in range(nc)], axis=0)
    eh, el = split(every)
    khv = kh[...].reshape(nc * rows, cdev)
    up = dot(jnp.concatenate([eh, el], axis=1), khv, 0, 0)
    gt = (
        up[:outs] + up[outs:] + dot(eh, kl[...].reshape(nc * rows, cdev), 0, 0)
    ) * sb_row

    def reduce_parts(part, send, rx, owned, xrx, full, ssem, rsem):
        mate = b + 1 - 2 * k2
        started = []
        for j in range(4):
            send[j] = part[:, j * piece : (j + 1) * piece]
        away = copy(
            send.at[pl.ds(2 * (1 - k2), 2)], rx, ssem.at[0], rsem.at[0], mate, c
        )
        away.start()
        started.append(away)
        yield
        away.wait_recv()
        owned[...] = send[pl.ds(2 * k2, 2)] + rx[...]
        for i in range(1, half):
            d = lax.rem(x + i, half) * 2 + k2
            out = copy(owned, xrx.at[x], ssem.at[i], rsem.at[1 + x], d, c)
            out.start()
            started.append(out)
        yield
        total = owned[...]
        for i in range(1, half):
            s = lax.rem(x + i, half)
            copy(owned, xrx.at[s], ssem.at[i], rsem.at[1 + s], s * 2 + k2, c).wait_recv()
            total = total + xrx[s]
        full[pl.ds(2 * k2, 2)] = total
        across = copy(
            full.at[pl.ds(2 * k2, 2)],
            full.at[pl.ds(2 * k2, 2)],
            ssem.at[half],
            rsem.at[1 + half],
            mate,
            c,
        )
        across.start()
        started.append(across)
        yield
        copy(
            full.at[pl.ds(2 * k2, 2)],
            full.at[pl.ds(2 * (1 - k2), 2)],
            ssem.at[half],
            rsem.at[1 + half],
            mate,
            c,
        ).wait_recv()
        yield
        for s in started:
            s.wait_send()
        yield

    def add_group(p):
        zs = z ^ p
        base = zs * group

        @pl.loop(1 if p == 0 else 0, group)
        def _(i):
            sb, sc = e_source(p * group + i)
            s = sc * nb + sb
            t = n - 1 - (p * group + i)
            copy(offsend.at[0], offrx.at[s], o_s.at[t], o_r.at[s], b, c).wait_recv()
            copy(packed.at[0, pl.ds(0, slots)], eigrx.at[s], e_s.at[t], e_r.at[s], b, c).wait_recv()

        mark = offrx[base]
        for i in range(1, group):
            mark = mark + offrx[base + i]
        sel = (
            (
                lax.broadcasted_iota(jnp.int32, (cdev, group * slots), 0) + 1
                == mark.astype(jnp.int32)
            )
            .astype(F32)
            .astype(LOW)
        )
        parts = split(eigrx[pl.ds(base, group)].reshape(group * slots, qb))
        return dot(
            jnp.concatenate([sel, sel], axis=1), jnp.concatenate(parts, axis=0), 1, 0
        )

    g_sum = reduce_parts(gt, gsend, grx, gown, gxrx, gall, g_s, g_r)
    next(g_sum)
    next(g_sum)
    ebar[...] = add_group(0)
    next(g_sum)
    ebar[...] += add_group(1)
    next(g_sum)

    def add_later(p):
        ebar[...] += add_group(p)

    for p in range(2, min(nz, 4)):
        add_later(p)
    for p in range(4, nz):
        add_later(p)

    g = jnp.concatenate([gall[j] for j in range(4)], axis=1)
    ebh, ebl = split(ebar[...])
    coeff = dot3(split(g), (ebh, ebl), 1, 0)
    og = outs // nc
    for j in range(nc):
        csend[j] = coeff[j * og : (j + 1) * og]

    def c_copy(t):
        d = at(lax.div(t, 2), lax.rem(t, 2))
        return copy(csend.at[d], crx.at[c], c_s.at[t], c_r.at[c], b, d)

    @pl.loop(1, nc)
    def _(t):
        c_copy(nc - t).start()

    crx[c] = csend[c]

    @pl.loop(1, nc)
    def _(t):
        s = at(lax.div(t, 2), lax.rem(t, 2))
        copy(csend.at[0], crx.at[s], c_s.at[t], c_r.at[s], b, s).wait_recv()

    csum = crx[0]
    for j in range(1, nc):
        csum = csum + crx[j]
    csum = csum * scale[b]
    cown[...] = csum
    call[c] = csum

    def ca_copy(t):
        return copy(
            cown, call.at[c], ca_s.at[t], ca_r.at[c], b, at(lax.div(t, 2), lax.rem(t, 2))
        )

    @pl.loop(1, nc)
    def _(t):
        ca_copy(nc - t).start()

    @pl.loop(1, nc)
    def _(t):
        s = at(lax.div(t, 2), lax.rem(t, 2))
        copy(cown, call.at[s], ca_s.at[t], ca_r.at[s], b, s).wait_recv()

    scaled = jnp.concatenate([call[j] for j in range(nc)], axis=0)
    u = dot3(split(scaled), (ebh, ebl), 1, 1)
    u_sum = reduce_parts(u, usend, urx, uown, uxrx, uall, u_s, u_r)
    for _ in range(4):
        next(u_sum)
    for j in range(4):
        upd_v[:, j * piece : (j + 1) * piece] = uall[j] - gall[j]
    upd_store = pltpu.make_async_copy(upd_v, upd_out, out_s.at[1])
    upd_store.start()

    spread_sent(feat, feat_all, f_s, f_r)

    @pl.loop(1, nc)
    def _(t):
        p_copy(t).wait_send()
        r_copy(t).wait_send()
        c_copy(t).wait_send()
        ca_copy(t).wait_send()

    @pl.loop(0, n - 1)
    def _(t):
        e_copy(t).wait_send()
        o_copy(t).wait_send()

    next(g_sum)
    next(u_sum)
    res_store.wait()
    upd_store.wait()


def per_device(
    pool_features,
    pool_targets,
    batch_index,
    centers,
    weights,
    eig_vectors,
    eig_scale,
    nys_owner,
    nys_offset,
):
    nb, nc = lax.axis_size("batch"), lax.axis_size("centers")
    n = nb * nc
    rows, (pool, dim) = batch_index.shape[0], pool_features.shape
    outs = pool_targets.shape[1]
    cdev = centers.shape[0]
    pts, q = eig_vectors.shape
    slots = max(2, 2 * pts // nc)
    group, half = 2 * nb, nb // 2
    qb, piece, og = q // nb, cdev // 4, outs // nc
    vm = pltpu.VMEM
    dma = pltpu.SemaphoreType.DMA
    spec = pl.BlockSpec(memory_space=pl.ANY)
    pair = [dma((nc,)), dma((nc,))]
    every = [dma((n,)), dma((n,))]
    sums = [dma((half + 1,)), dma((half + 2,))]
    reduced = [
        vm((4, outs, piece), F32),
        vm((2, outs, piece), F32),
        vm((2, outs, piece), F32),
        vm((half, 2, outs, piece), F32),
        vm((4, outs, piece), F32),
    ]
    residual, update = pl.pallas_call(
        functools.partial(body, nb, nc),
        out_shape=(
            jax.ShapeDtypeStruct((rows, outs), F32),
            jax.ShapeDtypeStruct((outs, cdev), F32),
        ),
        in_specs=[pl.BlockSpec(memory_space=pltpu.HBM)] * 9,
        out_specs=(spec, spec),
        scratch_shapes=[
            vm((pool, dim), F32),
            vm((outs, pool), F32),
            vm((1, rows), jnp.int32),
            pltpu.SMEM((1, rows), jnp.int32),
            vm((cdev, dim), F32),
            vm((outs, cdev), F32),
            vm((pts, q), F32),
            vm((nb, 1, qb), F32),
            vm((1, pts), jnp.int32),
            vm((1, pts), jnp.int32),
            vm((rows, outs), F32),
            vm((outs, cdev), F32),
            vm((rows, dim), F32),
            vm((nc, rows, dim), F32),
            vm((cdev, 4 * dim), LOW),
            vm((2 * outs, cdev), LOW),
            vm((nc // 2, 2 * rows, cdev), LOW),
            vm((nc // 2, 2 * rows, cdev), LOW),
            vm((nc, rows // 2, 2 * outs), F32),
            vm((nc, rows // 2, 2 * outs), F32),
            vm((rows // 2, 2 * outs), F32),
            vm((nc, rows // 2, 2 * outs), F32),
            vm((nb, nc * slots, qb), F32),
            vm((n, slots, qb), F32),
            vm((nc, 1, group * slots), F32),
            vm((n, 1, group * slots), F32),
            vm((cdev, qb), F32),
        ]
        + reduced
        + [
            vm((nc, og, qb), F32),
            vm((nc, og, qb), F32),
            vm((og, qb), F32),
            vm((nc, og, qb), F32),
        ]
        + reduced
        + [dma((10,)), dma((2,)), pltpu.SemaphoreType.REGULAR((2,))]
        + pair * 3
        + every * 2
        + sums
        + pair * 2
        + sums,
        compiler_params=pltpu.CompilerParams(
            collective_id=0, has_side_effects=True, vmem_limit_bytes=VMEM
        ),
    )(
        *(
            pltpu.with_memory_space_constraint(array, pltpu.HBM)
            for array in (
                pool_features,
                pool_targets.T,
                batch_index[None, :],
                centers,
                weights.T,
                eig_vectors,
                eig_scale.reshape(nb, 1, qb),
                nys_owner.reshape(1, pts),
                nys_offset[None, :],
            )
        )
    )
    return (residual, update.T)


def solution(mesh):
    placed = (
        P(("batch", "centers"), None),
        P(("batch", "centers"), None),
        P(("batch", "centers")),
        P("centers", None),
        P("centers", None),
        P(("batch", "centers"), None),
        P(),
        P(("batch", "centers"), None),
        P(("batch", "centers")),
    )
    return jax.shard_map(
        per_device,
        mesh=mesh,
        in_specs=placed,
        out_specs=(P(("batch", "centers"), None), P("centers", None)),
        check_vma=False,
    )
```

```python
import functools
import math

import jax
import jax.numpy as jnp
from jax import lax
from jax.experimental import pallas as pl
from jax.experimental.pallas import tpu as pltpu
from jax.sharding import PartitionSpec as P

DEPTH = 3
EPS = 1e-06
HIGH = lax.Precision.HIGHEST
VMEM = 32 * 2**20
MESH = pl.DeviceIdType.MESH
LOW = jnp.bfloat16
F32 = jnp.float32
INNER, OUTER = 8, 12
ACOS = (
    1.5707963050,
    -0.2145988016,
    0.0889789874,
    -0.0501743046,
    0.0308918810,
    -0.0170881256,
    0.0066700901,
    -0.0012624911,
)


def dot(a, b, ca, cb):
    return lax.dot_general(a, b, (((ca,), (cb,)), ((), ())), preferred_element_type=F32)


def exact(a, b, ca, cb):
    return lax.dot_general(
        a, b, (((ca,), (cb,)), ((), ())), precision=HIGH, preferred_element_type=F32
    )


def split(x):
    hi = x.astype(LOW)
    return hi, (x - hi.astype(F32)).astype(LOW)


def dot3(a, b, ca, cb):
    (ah, al), (bh, bl) = a, b
    rows = ah.shape[1 - ca]
    both = dot(jnp.concatenate([ah, al], axis=1 - ca), bh, ca, cb)
    return both[:rows] + both[rows:] + dot(ah, bl, ca, cb)


def fold(x):
    h = x.shape[0] // 2
    return jnp.concatenate([x[:h], x[h:]], axis=1)


def unfold(x):
    h = x.shape[1] // 2
    return jnp.concatenate([x[:, :h], x[:, h:]], axis=0)


def arc_parts(x):
    u = jnp.maximum(1.0 - x, 1e-30)
    poly = jnp.full_like(x, ACOS[-1] / math.pi)
    for a in ACOS[-2::-1]:
        poly = poly * x + a / math.pi
    v = u * (1.0 + x)
    return u * lax.rsqrt(u) * poly, v * lax.rsqrt(v) * (1.0 / math.pi)


def tangent_kernel(cosine):
    arc, sine = arc_parts(jnp.abs(cosine))
    remain = jnp.where(cosine < 0.0, arc, 1.0 - arc)
    prod = remain * cosine
    sigma = sine + prod
    tangent = sigma + prod
    for _ in range(DEPTH - 1):
        arc, sine = arc_parts(sigma)
        remain = 1.0 - arc
        sigma = sine + remain * sigma
        tangent = sigma + tangent * remain
    return tangent


def body(
    nb,
    nc,
    pool_f_h,
    pool_t_h,
    index_h,
    cen_h,
    wts_h,
    eig_h,
    scale_h,
    owner_h,
    offset_h,
    res_out,
    upd_out,
    pool_f,
    pool_t,
    index,
    index_s,
    cen,
    wts,
    eig,
    scale,
    owner,
    offset,
    res_v,
    upd_v,
    feat,
    feat_all,
    ccat,
    wcat,
    kh,
    kl,
    ppart,
    prx,
    rsend,
    rrx,
    packed,
    eigrx,
    offsend,
    offrx,
    ebar,
    gsend,
    grx,
    gown,
    gxrx,
    gall,
    csend,
    crx,
    cown,
    call,
    usend,
    urx,
    uown,
    uxrx,
    uall,
    in_s,
    out_s,
    told,
    f_s,
    f_r,
    p_s,
    p_r,
    r_s,
    r_r,
    e_s,
    e_r,
    o_s,
    o_r,
    g_s,
    g_r,
    c_s,
    c_r,
    ca_s,
    ca_r,
    u_s,
    u_r,
):
    b = lax.axis_index("batch")
    c = lax.axis_index("centers")
    n = nb * nc
    me = b * nc + c
    half = nb // 2
    k2, x = lax.rem(b, 2), lax.div(b, 2)
    z, y = lax.div(c, 2), lax.rem(c, 2)
    nz = nc // 2
    mine = c * nb + b
    rows, dim = feat.shape
    outs, cdev = wts.shape
    pts = owner.shape[1]
    group = 2 * nb
    slots = packed.shape[1] // nc
    qb = packed.shape[2]
    piece = cdev // 4
    rows_total = rows * n

    def copy(src, dst, ssem, rsem, db, dc):
        return pltpu.make_async_remote_copy(
            src_ref=src,
            dst_ref=dst,
            send_sem=ssem,
            recv_sem=rsem,
            device_id=(db, dc),
            device_id_type=MESH,
        )

    barrier = pltpu.get_barrier_semaphore()

    def greet(zd, first):
        @pl.loop(first, group)
        def _(i):
            o = lax.rem(b + (y * nb) + i, group)
            pl.semaphore_signal(
                barrier,
                inc=1,
                device_id=(lax.rem(o, nb), zd * 2 + lax.div(o, nb)),
                device_id_type=MESH,
            )

    greet(z, 1)

    @pl.when(z > 0)
    def _():
        greet(z - 1, 0)

    @pl.when(z < nz - 1)
    def _():
        greet(z + 1, 0)

    loads = [
        pltpu.make_async_copy(src, dst, in_s.at[i])
        for i, (src, dst) in enumerate(
            (
                (index_h, index_s),
                (pool_f_h, pool_f),
                (owner_h, owner),
                (offset_h, offset),
                (eig_h, eig),
                (cen_h, cen),
                (wts_h, wts),
                (scale_h, scale),
                (index_h, index),
                (pool_t_h, pool_t),
            )
        )
    ]
    for load in loads:
        load.start()

    loads[0].wait()
    loads[1].wait()

    @pl.loop(0, rows, unroll=8)
    def _(j):
        feat[pl.ds(j, 1), :] = pool_f[pl.ds(index_s[0, j], 1), :]

    feat_all[c] = feat[...]

    inner = jnp.logical_and(z > 0, z < nz - 1)

    @pl.when(inner)
    def _():
        pl.semaphore_wait(barrier, 3 * group - 1)

    @pl.when(jnp.logical_not(inner))
    def _():
        pl.semaphore_wait(barrier, 2 * group - 1)

    def at(zo, yo):
        return (z ^ zo) * 2 + (y ^ yo)

    mate = at(0, 1)

    def spread(src, dst, ssem, rsem, t):
        p, on = lax.div(t, 2), lax.rem(t, 2)
        s = at(p * on, 0)
        d = at(p * (1 - on), on)
        return copy(src if src is not None else dst.at[s], dst.at[s], ssem.at[t], rsem.at[s], b, d)

    def spread_pass(dst, ssem, rsem, p):
        s = at(p, 0)
        copy(dst.at[s], dst.at[s], ssem.at[0], rsem.at[s], b, s).wait_recv()
        spread(None, dst, ssem, rsem, 2 * p + 1).start()

    def spread_end(dst, ssem, rsem, p):
        s = at(p, 1)
        copy(dst.at[s], dst.at[s], ssem.at[0], rsem.at[s], b, s).wait_recv()

    def spread_sent(src, dst, ssem, rsem):
        spread(src, dst, ssem, rsem, 1).wait_send()

        @pl.loop(2, nc)
        def _(t):
            spread(None, dst, ssem, rsem, t).wait_send()

    def tell(which, zd):
        pl.semaphore_signal(
            told.at[which], inc=1, device_id=(b, zd * 2 + y), device_id_type=MESH
        )

    @pl.when(z == 1)
    def _():
        tell(0, z + 1)

    @pl.when(z == nz - 2)
    def _():
        tell(1, z - 1)

    @pl.loop(1, nz)
    def _(p):
        @pl.when(jnp.abs((z ^ p) - z) == 1)
        def _():
            spread(feat, feat_all, f_s, f_r, 2 * p).start()

    spread(feat, feat_all, f_s, f_r, 1).start()

    def hear():
        @pl.when(z >= 2)
        def _():
            pl.semaphore_wait(told.at[0], 1)

            @pl.when(z < nz - 1)
            def _():
                tell(0, z + 1)

        @pl.when(z <= nz - 3)
        def _():
            pl.semaphore_wait(told.at[1], 1)

            @pl.when(z > 0)
            def _():
                tell(1, z - 1)

        @pl.loop(1, nz)
        def _(i):
            p = nz - i

            @pl.when(jnp.abs((z ^ p) - z) > 1)
            def _():
                spread(feat, feat_all, f_s, f_r, 2 * p).start()

    @pl.when(z >= nz // 2)
    def _():
        hear()

    loads[2].wait()
    loads[3].wait()
    own = owner[...]
    hot = (own == lax.broadcasted_iota(jnp.int32, (nc, pts), 0)).astype(F32)
    upper = (
        lax.broadcasted_iota(jnp.int32, (pts, pts), 0)
        < lax.broadcasted_iota(jnp.int32, (pts, pts), 1)
    ).astype(F32)
    rank = jnp.sum(
        dot(hot.astype(LOW), upper.astype(LOW), 1, 0) * hot, axis=0, keepdims=True
    ).astype(jnp.int32)
    place = (
        (lax.broadcasted_iota(jnp.int32, (nc * slots, pts), 0) == own * slots + rank)
        .astype(F32)
        .astype(LOW)
    )
    loads[4].wait()
    both = jnp.concatenate(split(eig[...]), axis=0)
    place2 = jnp.concatenate([place, place], axis=1)
    for j in range(nb):
        packed[j] = dot(place2, both[:, j * qb : (j + 1) * qb], 1, 0)
    here = (
        lax.broadcasted_iota(jnp.int32, (group * slots, pts), 0)
        == (y * nb + b) * slots + rank
    ).astype(F32)
    marks = exact(hot * (offset[...].astype(F32) + 1.0), here, 1, 1)
    for j in range(nc):
        offsend[j] = marks[j : j + 1]
    eigrx[mine] = packed[b, pl.ds(pl.multiple_of(c * slots, slots), slots)]
    offrx[mine] = offsend[c]

    loads[5].wait()
    cval = cen[...]
    csq = cval * cval
    ncol = jnp.mean(csq, axis=1, keepdims=True) + EPS
    ch, cl = split(cval / (jnp.sqrt(ncol) * dim))
    ccat[...] = jnp.concatenate([ch, cl, ch, cl], axis=1)
    sb_row = jnp.sqrt(exact(jnp.full((8, dim), 1.0 / dim, F32), csq, 1, 1)[0:1] + EPS)
    loads[6].wait()
    wcat[...] = jnp.concatenate(split(wts[...] * sb_row), axis=0)

    @pl.when(z < nz // 2)
    def _():
        hear()

    def e_place(t):
        own_plane = t - (n - group) + 1
        far_first = jnp.where(t < n // 2, n - 1 - t, t - n // 2 + group)
        near_between = jnp.where(
            t < n // 4,
            n - 1 - t,
            jnp.where(
                t < 3 * n // 4 - group, t - n // 4 + group, n - 1 + n // 2 - group - t
            ),
        )
        o = jnp.where(t >= n - group, own_plane, jnp.where(inner, far_first, near_between))
        return lax.rem(b + lax.rem(o, nb), nb), at(lax.div(o, group), lax.rem(lax.div(o, nb), 2))

    def e_source(o):
        return lax.rem(b - lax.rem(o, nb) + nb, nb), at(
            lax.div(o, group), lax.rem(lax.div(o, nb), 2)
        )

    def e_copy(t):
        db, dc = e_place(t)
        return copy(
            packed.at[db, pl.ds(pl.multiple_of(dc * slots, slots), slots)],
            eigrx.at[mine],
            e_s.at[t],
            e_r.at[mine],
            db,
            dc,
        )

    def o_copy(t):
        db, dc = e_place(t)
        return copy(offsend.at[dc], offrx.at[mine], o_s.at[t], o_r.at[mine], db, dc)

    early = jnp.where(inner, INNER * (n - group) // 24, OUTER * (n - group) // 24)

    def e_start(lo, hi):
        @pl.loop(lo, hi)
        def _(t):
            e_copy(t).start()

    e_start(n - group, n - 1)
    e_start(0, early)

    def p_copy(t):
        s = at(lax.div(t, 2), lax.rem(t, 2))
        return copy(ppart.at[s], prx.at[c], p_s.at[t], p_r.at[c], b, s)

    def pair(p):
        zs = z ^ p
        av = feat_all[pl.ds(zs * 2, 2)].reshape(2 * rows, dim)
        na = jnp.mean(av * av, axis=1, keepdims=True) + EPS
        ah, al = split(av * lax.rsqrt(na))
        k = tangent_kernel(dot(jnp.concatenate([ah, ah, al, al], axis=1), ccat[...], 1, 1))
        hi, lo = split(k)
        kh[zs] = hi
        kl[zs] = lo
        top = dot(hi, wcat[...], 1, 1)
        pred = top[:, :outs] + top[:, outs:] + dot(lo, wcat[:outs], 1, 1)
        return fold(pred[:rows]), fold(pred[rows:])

    spread_end(feat_all, f_s, f_r, 0)
    spread_pass(feat_all, f_s, f_r, 1)
    low, high = pair(0)
    prx[c] = jnp.where(y == 0, low, high)
    ppart[c ^ 1] = jnp.where(y == 0, high, low)
    p_copy(1).start()

    def later(p):
        spread_end(feat_all, f_s, f_r, p)
        lo, hi = pair(p)
        zs = (z ^ p) * 2
        ppart[zs] = lo
        ppart[zs + 1] = hi
        p_copy(2 * p).start()
        p_copy(2 * p + 1).start()

    spread_pass(feat_all, f_s, f_r, 2)
    later(1)
    spread_pass(feat_all, f_s, f_r, 3)
    later(2)

    @pl.loop(3, nz - 1)
    def _(p):
        spread_pass(feat_all, f_s, f_r, p + 1)
        later(p)

    later(nz - 1)

    @pl.loop(0, n - 1)
    def _(t):
        o_copy(t).start()

    a = feat[...]
    sa = jnp.sqrt(jnp.mean(a * a, axis=1, keepdims=True) + EPS)
    loads[7].wait()
    loads[8].wait()
    loads[9].wait()
    drawn = (
        (lax.broadcasted_iota(jnp.int32, (pool_t.shape[1], rows), 0) == index[...])
        .astype(F32)
        .astype(LOW)
    )
    th, tl = split(pool_t[...])
    picked = dot(jnp.concatenate([th, tl], axis=0), drawn, 1, 0)
    targ = (picked[:outs] + picked[outs:]).T

    @pl.loop(1, nc)
    def _(t):
        s = at(lax.div(t, 2), lax.rem(t, 2))
        copy(ppart.at[s], prx.at[s], p_s.at[t], p_r.at[s], b, s).wait_recv()

    pred = prx[0]
    for j in range(1, nc):
        pred = pred + prx[j]
    resid = unfold(pred) * sa - targ
    folded = fold(resid * (sa / math.sqrt(rows_total)))
    rsend[...] = folded
    rrx[c] = folded

    def r_copy(t):
        return copy(
            rsend, rrx.at[c], r_s.at[t], r_r.at[c], b, at(lax.div(t, 2), lax.rem(t, 2))
        )

    @pl.loop(1, nc)
    def _(t):
        r_copy(nc - t).start()

    e_start(early, n - group)

    res_v[...] = resid
    res_store = pltpu.make_async_copy(res_v, res_out, out_s.at[0])
    res_store.start()

    @pl.loop(1, nc)
    def _(t):
        s = at(lax.div(t, 2), lax.rem(t, 2))
        copy(rsend, rrx.at[s], r_s.at[t], r_r.at[s], b, s).wait_recv()

    every = jnp.concatenate([unfold(rrx[j]) for j in range(nc)], axis=0)
    eh, el = split(every)
    khv = kh[...].reshape(nc * rows, cdev)
    up = dot(jnp.concatenate([eh, el], axis=1), khv, 0, 0)
    gt = (
        up[:outs] + up[outs:] + dot(eh, kl[...].reshape(nc * rows, cdev), 0, 0)
    ) * sb_row

    def reduce_parts(part, send, rx, owned, xrx, full, ssem, rsem):
        mate = b + 1 - 2 * k2
        started = []
        for j in range(4):
            send[j] = part[:, j * piece : (j + 1) * piece]
        away = copy(
            send.at[pl.ds(2 * (1 - k2), 2)], rx, ssem.at[0], rsem.at[0], mate, c
        )
        away.start()
        started.append(away)
        yield
        away.wait_recv()
        owned[...] = send[pl.ds(2 * k2, 2)] + rx[...]
        for i in range(1, half):
            d = lax.rem(x + i, half) * 2 + k2
            out = copy(owned, xrx.at[x], ssem.at[i], rsem.at[1 + x], d, c)
            out.start()
            started.append(out)
        yield
        total = owned[...]
        for i in range(1, half):
            s = lax.rem(x + i, half)
            copy(owned, xrx.at[s], ssem.at[i], rsem.at[1 + s], s * 2 + k2, c).wait_recv()
            total = total + xrx[s]
        full[pl.ds(2 * k2, 2)] = total
        across = copy(
            full.at[pl.ds(2 * k2, 2)],
            full.at[pl.ds(2 * k2, 2)],
            ssem.at[half],
            rsem.at[1 + half],
            mate,
            c,
        )
        across.start()
        started.append(across)
        yield
        copy(
            full.at[pl.ds(2 * k2, 2)],
            full.at[pl.ds(2 * (1 - k2), 2)],
            ssem.at[half],
            rsem.at[1 + half],
            mate,
            c,
        ).wait_recv()
        yield
        for s in started:
            s.wait_send()
        yield

    def add_group(p):
        zs = z ^ p
        base = zs * group

        @pl.loop(1 if p == 0 else 0, group)
        def _(i):
            sb, sc = e_source(p * group + i)
            s = sc * nb + sb
            t = n - 1 - (p * group + i)
            copy(offsend.at[0], offrx.at[s], o_s.at[t], o_r.at[s], b, c).wait_recv()
            copy(packed.at[0, pl.ds(0, slots)], eigrx.at[s], e_s.at[t], e_r.at[s], b, c).wait_recv()

        mark = offrx[base]
        for i in range(1, group):
            mark = mark + offrx[base + i]
        sel = (
            (
                lax.broadcasted_iota(jnp.int32, (cdev, group * slots), 0) + 1
                == mark.astype(jnp.int32)
            )
            .astype(F32)
            .astype(LOW)
        )
        parts = split(eigrx[pl.ds(base, group)].reshape(group * slots, qb))
        return dot(
            jnp.concatenate([sel, sel], axis=1), jnp.concatenate(parts, axis=0), 1, 0
        )

    g_sum = reduce_parts(gt, gsend, grx, gown, gxrx, gall, g_s, g_r)
    next(g_sum)
    next(g_sum)
    ebar[...] = add_group(0)
    next(g_sum)
    next(g_sum)
    gsplit = split(jnp.concatenate([gall[j] for j in range(4)], axis=1))

    for p in range(nz - 1, 0, -1):
        ebar[...] += add_group(p)

    ebh, ebl = split(ebar[...])
    coeff = dot3(gsplit, (ebh, ebl), 1, 0)
    og = outs // nc
    for j in range(nc):
        csend[j] = coeff[j * og : (j + 1) * og]

    def c_copy(t):
        d = at(lax.div(t, 2), lax.rem(t, 2))
        return copy(csend.at[d], crx.at[c], c_s.at[t], c_r.at[c], b, d)

    @pl.loop(1, nc)
    def _(t):
        c_copy(nc - t).start()

    crx[c] = csend[c]

    @pl.loop(1, nc)
    def _(t):
        s = at(lax.div(t, 2), lax.rem(t, 2))
        copy(csend.at[0], crx.at[s], c_s.at[t], c_r.at[s], b, s).wait_recv()

    csum = crx[0]
    for j in range(1, nc):
        csum = csum + crx[j]
    csum = csum * scale[b]
    cown[...] = csum
    call[c] = csum

    def ca_copy(t):
        return copy(
            cown, call.at[c], ca_s.at[t], ca_r.at[c], b, at(lax.div(t, 2), lax.rem(t, 2))
        )

    @pl.loop(1, nc)
    def _(t):
        ca_copy(nc - t).start()

    @pl.loop(1, nc)
    def _(t):
        s = at(lax.div(t, 2), lax.rem(t, 2))
        copy(cown, call.at[s], ca_s.at[t], ca_r.at[s], b, s).wait_recv()

    scaled = jnp.concatenate([call[j] for j in range(nc)], axis=0)
    u = dot3(split(scaled), (ebh, ebl), 1, 1)
    u_sum = reduce_parts(u, usend, urx, uown, uxrx, uall, u_s, u_r)
    for _ in range(4):
        next(u_sum)
    for j in range(4):
        upd_v[:, j * piece : (j + 1) * piece] = uall[j] - gall[j]
    upd_store = pltpu.make_async_copy(upd_v, upd_out, out_s.at[1])
    upd_store.start()

    spread_sent(feat, feat_all, f_s, f_r)

    @pl.loop(1, nc)
    def _(t):
        p_copy(t).wait_send()
        r_copy(t).wait_send()
        c_copy(t).wait_send()
        ca_copy(t).wait_send()

    @pl.loop(0, n - 1)
    def _(t):
        e_copy(t).wait_send()
        o_copy(t).wait_send()

    next(g_sum)
    next(u_sum)
    res_store.wait()
    upd_store.wait()


def per_device(
    pool_features,
    pool_targets,
    batch_index,
    centers,
    weights,
    eig_vectors,
    eig_scale,
    nys_owner,
    nys_offset,
):
    nb, nc = lax.axis_size("batch"), lax.axis_size("centers")
    n = nb * nc
    rows, (pool, dim) = batch_index.shape[0], pool_features.shape
    outs = pool_targets.shape[1]
    cdev = centers.shape[0]
    pts, q = eig_vectors.shape
    slots = max(2, 2 * pts // nc)
    group, half = 2 * nb, nb // 2
    qb, piece, og = q // nb, cdev // 4, outs // nc
    vm = pltpu.VMEM
    dma = pltpu.SemaphoreType.DMA
    spec = pl.BlockSpec(memory_space=pl.ANY)
    pair = [dma((nc,)), dma((nc,))]
    every = [dma((n,)), dma((n,))]
    sums = [dma((half + 1,)), dma((half + 2,))]
    reduced = [
        vm((4, outs, piece), F32),
        vm((2, outs, piece), F32),
        vm((2, outs, piece), F32),
        vm((half, 2, outs, piece), F32),
        vm((4, outs, piece), F32),
    ]
    residual, update = pl.pallas_call(
        functools.partial(body, nb, nc),
        out_shape=(
            jax.ShapeDtypeStruct((rows, outs), F32),
            jax.ShapeDtypeStruct((outs, cdev), F32),
        ),
        in_specs=[pl.BlockSpec(memory_space=pltpu.HBM)] * 9,
        out_specs=(spec, spec),
        scratch_shapes=[
            vm((pool, dim), F32),
            vm((outs, pool), F32),
            vm((1, rows), jnp.int32),
            pltpu.SMEM((1, rows), jnp.int32),
            vm((cdev, dim), F32),
            vm((outs, cdev), F32),
            vm((pts, q), F32),
            vm((nb, 1, qb), F32),
            vm((1, pts), jnp.int32),
            vm((1, pts), jnp.int32),
            vm((rows, outs), F32),
            vm((outs, cdev), F32),
            vm((rows, dim), F32),
            vm((nc, rows, dim), F32),
            vm((cdev, 4 * dim), LOW),
            vm((2 * outs, cdev), LOW),
            vm((nc // 2, 2 * rows, cdev), LOW),
            vm((nc // 2, 2 * rows, cdev), LOW),
            vm((nc, rows // 2, 2 * outs), F32),
            vm((nc, rows // 2, 2 * outs), F32),
            vm((rows // 2, 2 * outs), F32),
            vm((nc, rows // 2, 2 * outs), F32),
            vm((nb, nc * slots, qb), F32),
            vm((n, slots, qb), F32),
            vm((nc, 1, group * slots), F32),
            vm((n, 1, group * slots), F32),
            vm((cdev, qb), F32),
        ]
        + reduced
        + [
            vm((nc, og, qb), F32),
            vm((nc, og, qb), F32),
            vm((og, qb), F32),
            vm((nc, og, qb), F32),
        ]
        + reduced
        + [dma((10,)), dma((2,)), pltpu.SemaphoreType.REGULAR((2,))]
        + pair * 3
        + every * 2
        + sums
        + pair * 2
        + sums,
        compiler_params=pltpu.CompilerParams(
            collective_id=0, has_side_effects=True, vmem_limit_bytes=VMEM
        ),
    )(
        *(
            pltpu.with_memory_space_constraint(array, pltpu.HBM)
            for array in (
                pool_features,
                pool_targets.T,
                batch_index[None, :],
                centers,
                weights.T,
                eig_vectors,
                eig_scale.reshape(nb, 1, qb),
                nys_owner.reshape(1, pts),
                nys_offset[None, :],
            )
        )
    )
    return (residual, update.T)


def solution(mesh):
    placed = (
        P(("batch", "centers"), None),
        P(("batch", "centers"), None),
        P(("batch", "centers")),
        P("centers", None),
        P("centers", None),
        P(("batch", "centers"), None),
        P(),
        P(("batch", "centers"), None),
        P(("batch", "centers")),
    )
    return jax.shard_map(
        per_device,
        mesh=mesh,
        in_specs=placed,
        out_specs=(P(("batch", "centers"), None), P("centers", None)),
        check_vma=False,
    )
```

```python
import functools
import math

import jax
import jax.numpy as jnp
from jax import lax
from jax.experimental import pallas as pl
from jax.experimental.pallas import tpu as pltpu
from jax.sharding import PartitionSpec as P

DEPTH = 3
EPS = 1e-06
HIGH = lax.Precision.HIGHEST
VMEM = 32 * 2**20
MESH = pl.DeviceIdType.MESH
LOW = jnp.bfloat16
F32 = jnp.float32
INNER, OUTER = 8, 12
ACOS = (
    1.5707963050,
    -0.2145988016,
    0.0889789874,
    -0.0501743046,
    0.0308918810,
    -0.0170881256,
    0.0066700901,
    -0.0012624911,
)


def dot(a, b, ca, cb):
    return lax.dot_general(a, b, (((ca,), (cb,)), ((), ())), preferred_element_type=F32)


def exact(a, b, ca, cb):
    return lax.dot_general(
        a, b, (((ca,), (cb,)), ((), ())), precision=HIGH, preferred_element_type=F32
    )


def split(x):
    hi = x.astype(LOW)
    return hi, (x - hi.astype(F32)).astype(LOW)


def dot3(a, b, ca, cb):
    (ah, al), (bh, bl) = a, b
    rows = ah.shape[1 - ca]
    both = dot(jnp.concatenate([ah, al], axis=1 - ca), bh, ca, cb)
    return both[:rows] + both[rows:] + dot(ah, bl, ca, cb)


def fold(x):
    h = x.shape[0] // 2
    return jnp.concatenate([x[:h], x[h:]], axis=1)


def unfold(x):
    h = x.shape[1] // 2
    return jnp.concatenate([x[:, :h], x[:, h:]], axis=0)


def arc_parts(x):
    u = jnp.maximum(1.0 - x, 1e-30)
    poly = jnp.full_like(x, ACOS[-1] / math.pi)
    for a in ACOS[-2::-1]:
        poly = poly * x + a / math.pi
    v = u * (1.0 + x)
    return u * lax.rsqrt(u) * poly, v * lax.rsqrt(v) * (1.0 / math.pi)


def tangent_kernel(cosine):
    arc, sine = arc_parts(jnp.abs(cosine))
    remain = jnp.where(cosine < 0.0, arc, 1.0 - arc)
    prod = remain * cosine
    sigma = sine + prod
    tangent = sigma + prod
    for _ in range(DEPTH - 1):
        arc, sine = arc_parts(sigma)
        remain = 1.0 - arc
        sigma = sine + remain * sigma
        tangent = sigma + tangent * remain
    return tangent


def body(
    nb,
    nc,
    pool_f_h,
    pool_t_h,
    index_h,
    cen_h,
    wts_h,
    eig_h,
    scale_h,
    owner_h,
    offset_h,
    res_out,
    upd_out,
    pool_f,
    pool_t,
    index,
    index_s,
    cen,
    wts,
    eig,
    scale,
    owner,
    offset,
    res_v,
    upd_v,
    feat,
    feat_all,
    ccat,
    wcat,
    kh,
    kl,
    ppart,
    prx,
    rsend,
    rrx,
    packed,
    eigrx,
    offsend,
    offrx,
    ebar,
    gsend,
    grx,
    gown,
    gxrx,
    gall,
    csend,
    crx,
    cown,
    call,
    usend,
    urx,
    uown,
    uxrx,
    uall,
    in_s,
    out_s,
    told,
    f_s,
    f_r,
    p_s,
    p_r,
    r_s,
    r_r,
    e_s,
    e_r,
    o_s,
    o_r,
    g_s,
    g_r,
    c_s,
    c_r,
    ca_s,
    ca_r,
    u_s,
    u_r,
):
    b = lax.axis_index("batch")
    c = lax.axis_index("centers")
    n = nb * nc
    me = b * nc + c
    half = nb // 2
    k2, x = lax.rem(b, 2), lax.div(b, 2)
    z, y = lax.div(c, 2), lax.rem(c, 2)
    nz = nc // 2
    mine = c * nb + b
    rows, dim = feat.shape
    outs, cdev = wts.shape
    pts = owner.shape[1]
    group = 2 * nb
    slots = packed.shape[1] // nc
    qb = packed.shape[2]
    piece = cdev // 4
    rows_total = rows * n

    def copy(src, dst, ssem, rsem, db, dc):
        return pltpu.make_async_remote_copy(
            src_ref=src,
            dst_ref=dst,
            send_sem=ssem,
            recv_sem=rsem,
            device_id=(db, dc),
            device_id_type=MESH,
        )

    barrier = pltpu.get_barrier_semaphore()

    def greet(zd, first):
        @pl.loop(first, group)
        def _(i):
            o = lax.rem(b + (y * nb) + i, group)
            pl.semaphore_signal(
                barrier,
                inc=1,
                device_id=(lax.rem(o, nb), zd * 2 + lax.div(o, nb)),
                device_id_type=MESH,
            )

    greet(z, 1)

    @pl.when(z > 0)
    def _():
        greet(z - 1, 0)

    @pl.when(z < nz - 1)
    def _():
        greet(z + 1, 0)

    loads = [
        pltpu.make_async_copy(src, dst, in_s.at[i])
        for i, (src, dst) in enumerate(
            (
                (index_h, index_s),
                (pool_f_h, pool_f),
                (owner_h, owner),
                (offset_h, offset),
                (eig_h, eig),
                (cen_h, cen),
                (wts_h, wts),
                (scale_h, scale),
                (index_h, index),
                (pool_t_h, pool_t),
            )
        )
    ]
    for load in loads:
        load.start()

    loads[0].wait()
    loads[1].wait()

    @pl.loop(0, rows, unroll=8)
    def _(j):
        feat[pl.ds(j, 1), :] = pool_f[pl.ds(index_s[0, j], 1), :]

    feat_all[c] = feat[...]

    inner = jnp.logical_and(z > 0, z < nz - 1)

    @pl.when(inner)
    def _():
        pl.semaphore_wait(barrier, 3 * group - 1)

    @pl.when(jnp.logical_not(inner))
    def _():
        pl.semaphore_wait(barrier, 2 * group - 1)

    def at(zo, yo):
        return (z ^ zo) * 2 + (y ^ yo)

    mate = at(0, 1)

    def spread(src, dst, ssem, rsem, t):
        p, on = lax.div(t, 2), lax.rem(t, 2)
        s = at(p * on, 0)
        d = at(p * (1 - on), on)
        return copy(src if src is not None else dst.at[s], dst.at[s], ssem.at[t], rsem.at[s], b, d)

    def spread_pass(dst, ssem, rsem, p):
        s = at(p, 0)
        copy(dst.at[s], dst.at[s], ssem.at[0], rsem.at[s], b, s).wait_recv()
        spread(None, dst, ssem, rsem, 2 * p + 1).start()

    def spread_end(dst, ssem, rsem, p):
        s = at(p, 1)
        copy(dst.at[s], dst.at[s], ssem.at[0], rsem.at[s], b, s).wait_recv()

    def spread_sent(src, dst, ssem, rsem):
        spread(src, dst, ssem, rsem, 1).wait_send()

        @pl.loop(2, nc)
        def _(t):
            spread(None, dst, ssem, rsem, t).wait_send()

    def tell(which, zd):
        pl.semaphore_signal(
            told.at[which], inc=1, device_id=(b, zd * 2 + y), device_id_type=MESH
        )

    @pl.when(z == 1)
    def _():
        tell(0, z + 1)

    @pl.when(z == nz - 2)
    def _():
        tell(1, z - 1)

    @pl.loop(1, nz)
    def _(p):
        @pl.when(jnp.abs((z ^ p) - z) == 1)
        def _():
            spread(feat, feat_all, f_s, f_r, 2 * p).start()

    spread(feat, feat_all, f_s, f_r, 1).start()

    def hear():
        @pl.when(z >= 2)
        def _():
            pl.semaphore_wait(told.at[0], 1)

            @pl.when(z < nz - 1)
            def _():
                tell(0, z + 1)

        @pl.when(z <= nz - 3)
        def _():
            pl.semaphore_wait(told.at[1], 1)

            @pl.when(z > 0)
            def _():
                tell(1, z - 1)

        @pl.loop(1, nz)
        def _(i):
            p = nz - i

            @pl.when(jnp.abs((z ^ p) - z) > 1)
            def _():
                spread(feat, feat_all, f_s, f_r, 2 * p).start()

    @pl.when(z >= nz // 2)
    def _():
        hear()

    loads[2].wait()
    loads[3].wait()
    own = owner[...]
    hot = (own == lax.broadcasted_iota(jnp.int32, (nc, pts), 0)).astype(F32)
    upper = (
        lax.broadcasted_iota(jnp.int32, (pts, pts), 0)
        < lax.broadcasted_iota(jnp.int32, (pts, pts), 1)
    ).astype(F32)
    rank = jnp.sum(
        dot(hot.astype(LOW), upper.astype(LOW), 1, 0) * hot, axis=0, keepdims=True
    ).astype(jnp.int32)
    place = (
        (lax.broadcasted_iota(jnp.int32, (nc * slots, pts), 0) == own * slots + rank)
        .astype(F32)
        .astype(LOW)
    )
    loads[4].wait()
    both = jnp.concatenate(split(eig[...]), axis=0)
    place2 = jnp.concatenate([place, place], axis=1)
    for j in range(nb):
        packed[j] = dot(place2, both[:, j * qb : (j + 1) * qb], 1, 0)
    here = (
        lax.broadcasted_iota(jnp.int32, (group * slots, pts), 0)
        == (y * nb + b) * slots + rank
    ).astype(F32)
    marks = exact(hot * (offset[...].astype(F32) + 1.0), here, 1, 1)
    for j in range(nc):
        offsend[j] = marks[j : j + 1]
    eigrx[mine] = packed[b, pl.ds(pl.multiple_of(c * slots, slots), slots)]
    offrx[mine] = offsend[c]

    loads[5].wait()
    cval = cen[...]
    csq = cval * cval
    ncol = jnp.mean(csq, axis=1, keepdims=True) + EPS
    ch, cl = split(cval / (jnp.sqrt(ncol) * dim))
    ccat[...] = jnp.concatenate([ch, cl, ch, cl], axis=1)
    sb_row = jnp.sqrt(exact(jnp.full((8, dim), 1.0 / dim, F32), csq, 1, 1)[0:1] + EPS)
    loads[6].wait()
    wcat[...] = jnp.concatenate(split(wts[...] * sb_row), axis=0)

    @pl.when(z < nz // 2)
    def _():
        hear()

    def e_place(t):
        own_plane = t - (n - group) + 1
        far_first = jnp.where(t < n // 2, n - 1 - t, t - n // 2 + group)
        near_between = jnp.where(
            t < n // 4,
            n - 1 - t,
            jnp.where(
                t < 3 * n // 4 - group, t - n // 4 + group, n - 1 + n // 2 - group - t
            ),
        )
        o = jnp.where(t >= n - group, own_plane, jnp.where(inner, far_first, near_between))
        return lax.rem(b + lax.rem(o, nb), nb), at(lax.div(o, group), lax.rem(lax.div(o, nb), 2))

    def e_source(o):
        return lax.rem(b - lax.rem(o, nb) + nb, nb), at(
            lax.div(o, group), lax.rem(lax.div(o, nb), 2)
        )

    def e_copy(t):
        db, dc = e_place(t)
        return copy(
            packed.at[db, pl.ds(pl.multiple_of(dc * slots, slots), slots)],
            eigrx.at[mine],
            e_s.at[t],
            e_r.at[mine],
            db,
            dc,
        )

    def o_copy(t):
        db, dc = e_place(t)
        return copy(offsend.at[dc], offrx.at[mine], o_s.at[t], o_r.at[mine], db, dc)

    early = jnp.where(inner, INNER * (n - group) // 24, OUTER * (n - group) // 24)

    def e_start(lo, hi):
        @pl.loop(lo, hi)
        def _(t):
            e_copy(t).start()

    e_start(n - group, n - 1)
    e_start(0, early)

    def p_copy(t):
        s = at(lax.div(t, 2), lax.rem(t, 2))
        return copy(ppart.at[s], prx.at[c], p_s.at[t], p_r.at[c], b, s)

    def pair(p):
        zs = z ^ p
        av = feat_all[pl.ds(zs * 2, 2)].reshape(2 * rows, dim)
        na = jnp.mean(av * av, axis=1, keepdims=True) + EPS
        ah, al = split(av * lax.rsqrt(na))
        k = tangent_kernel(dot(jnp.concatenate([ah, ah, al, al], axis=1), ccat[...], 1, 1))
        hi, lo = split(k)
        kh[zs] = hi
        kl[zs] = lo
        top = dot(hi, wcat[...], 1, 1)
        pred = top[:, :outs] + top[:, outs:] + dot(lo, wcat[:outs], 1, 1)
        return fold(pred[:rows]), fold(pred[rows:])

    spread_end(feat_all, f_s, f_r, 0)
    spread_pass(feat_all, f_s, f_r, 1)
    low, high = pair(0)
    prx[c] = jnp.where(y == 0, low, high)
    ppart[c ^ 1] = jnp.where(y == 0, high, low)
    p_copy(1).start()

    def later(p):
        spread_end(feat_all, f_s, f_r, p)
        lo, hi = pair(p)
        zs = (z ^ p) * 2
        ppart[zs] = lo
        ppart[zs + 1] = hi
        p_copy(2 * p).start()
        p_copy(2 * p + 1).start()

    spread_pass(feat_all, f_s, f_r, 2)
    later(1)
    spread_pass(feat_all, f_s, f_r, 3)
    later(2)

    @pl.loop(3, nz - 1)
    def _(p):
        spread_pass(feat_all, f_s, f_r, p + 1)
        later(p)

    later(nz - 1)

    @pl.loop(0, n - 1)
    def _(t):
        o_copy(t).start()

    a = feat[...]
    sa = jnp.sqrt(jnp.mean(a * a, axis=1, keepdims=True) + EPS)
    loads[7].wait()
    loads[8].wait()
    loads[9].wait()
    drawn = (
        (lax.broadcasted_iota(jnp.int32, (pool_t.shape[1], rows), 0) == index[...])
        .astype(F32)
        .astype(LOW)
    )
    th, tl = split(pool_t[...])
    picked = dot(jnp.concatenate([th, tl], axis=0), drawn, 1, 0)
    targ = (picked[:outs] + picked[outs:]).T

    @pl.loop(1, nc)
    def _(t):
        s = at(lax.div(t, 2), lax.rem(t, 2))
        copy(ppart.at[s], prx.at[s], p_s.at[t], p_r.at[s], b, s).wait_recv()

    pred = prx[0]
    for j in range(1, nc):
        pred = pred + prx[j]
    resid = unfold(pred) * sa - targ
    folded = fold(resid * (sa / math.sqrt(rows_total)))
    rsend[...] = folded
    rrx[c] = folded

    def r_copy(t):
        return copy(
            rsend, rrx.at[c], r_s.at[t], r_r.at[c], b, at(lax.div(t, 2), lax.rem(t, 2))
        )

    @pl.loop(1, nc)
    def _(t):
        r_copy(nc - t).start()

    e_start(early, n - group)

    res_v[...] = resid
    res_store = pltpu.make_async_copy(res_v, res_out, out_s.at[0])
    res_store.start()

    @pl.loop(1, nc)
    def _(t):
        s = at(lax.div(t, 2), lax.rem(t, 2))
        copy(rsend, rrx.at[s], r_s.at[t], r_r.at[s], b, s).wait_recv()

    every = jnp.concatenate([unfold(rrx[j]) for j in range(nc)], axis=0)
    eh, el = split(every)
    khv = kh[...].reshape(nc * rows, cdev)
    up = dot(jnp.concatenate([eh, el], axis=1), khv, 0, 0)
    gt = (
        up[:outs] + up[outs:] + dot(eh, kl[...].reshape(nc * rows, cdev), 0, 0)
    ) * sb_row

    def reduce_parts(part, send, rx, owned, xrx, full, ssem, rsem):
        mate = b + 1 - 2 * k2
        started = []
        for j in range(4):
            send[j] = part[:, j * piece : (j + 1) * piece]
        away = copy(
            send.at[pl.ds(2 * (1 - k2), 2)], rx, ssem.at[0], rsem.at[0], mate, c
        )
        away.start()
        started.append(away)
        yield
        away.wait_recv()
        owned[...] = send[pl.ds(2 * k2, 2)] + rx[...]
        for i in range(1, half):
            d = lax.rem(x + i, half) * 2 + k2
            out = copy(owned, xrx.at[x], ssem.at[i], rsem.at[1 + x], d, c)
            out.start()
            started.append(out)
        yield
        total = owned[...]
        for i in range(1, half):
            s = lax.rem(x + i, half)
            copy(owned, xrx.at[s], ssem.at[i], rsem.at[1 + s], s * 2 + k2, c).wait_recv()
            total = total + xrx[s]
        full[pl.ds(2 * k2, 2)] = total
        across = copy(
            full.at[pl.ds(2 * k2, 2)],
            full.at[pl.ds(2 * k2, 2)],
            ssem.at[half],
            rsem.at[1 + half],
            mate,
            c,
        )
        across.start()
        started.append(across)
        yield
        copy(
            full.at[pl.ds(2 * k2, 2)],
            full.at[pl.ds(2 * (1 - k2), 2)],
            ssem.at[half],
            rsem.at[1 + half],
            mate,
            c,
        ).wait_recv()
        yield
        for s in started:
            s.wait_send()
        yield

    def add_group(p):
        zs = z ^ p
        base = zs * group

        @pl.loop(1 if p == 0 else 0, group)
        def _(i):
            sb, sc = e_source(p * group + i)
            s = sc * nb + sb
            t = n - 1 - (p * group + i)
            copy(offsend.at[0], offrx.at[s], o_s.at[t], o_r.at[s], b, c).wait_recv()
            copy(packed.at[0, pl.ds(0, slots)], eigrx.at[s], e_s.at[t], e_r.at[s], b, c).wait_recv()

        mark = offrx[base]
        for i in range(1, group):
            mark = mark + offrx[base + i]
        sel = (
            (
                lax.broadcasted_iota(jnp.int32, (cdev, group * slots), 0) + 1
                == mark.astype(jnp.int32)
            )
            .astype(F32)
            .astype(LOW)
        )
        parts = split(eigrx[pl.ds(base, group)].reshape(group * slots, qb))
        return dot(
            jnp.concatenate([sel, sel], axis=1), jnp.concatenate(parts, axis=0), 1, 0
        )

    g_sum = reduce_parts(gt, gsend, grx, gown, gxrx, gall, g_s, g_r)
    next(g_sum)
    next(g_sum)
    ebar[...] = add_group(0)
    next(g_sum)
    next(g_sum)
    gsplit = split(jnp.concatenate([gall[j] for j in range(4)], axis=1))

    for p in range(nz - 1, 0, -1):
        ebar[...] += add_group(p)

    ebh, ebl = split(ebar[...])
    coeff = dot3(gsplit, (ebh, ebl), 1, 0)
    og = outs // nc
    for j in range(nc):
        csend[j] = coeff[j * og : (j + 1) * og]

    def c_copy(t):
        d = at(lax.div(t, 2), lax.rem(t, 2))
        return copy(csend.at[d], crx.at[c], c_s.at[t], c_r.at[c], b, d)

    @pl.loop(1, nc)
    def _(t):
        c_copy(nc - t).start()

    crx[c] = csend[c]

    @pl.loop(1, nc)
    def _(t):
        s = at(lax.div(t, 2), lax.rem(t, 2))
        copy(csend.at[0], crx.at[s], c_s.at[t], c_r.at[s], b, s).wait_recv()

    csum = crx[0]
    for j in range(1, nc):
        csum = csum + crx[j]
    csum = csum * scale[b]
    cown[...] = csum
    call[c] = csum

    def ca_copy(t):
        return copy(
            cown, call.at[c], ca_s.at[t], ca_r.at[c], b, at(lax.div(t, 2), lax.rem(t, 2))
        )

    @pl.loop(1, nc)
    def _(t):
        ca_copy(nc - t).start()

    @pl.loop(1, nc)
    def _(t):
        s = at(lax.div(t, 2), lax.rem(t, 2))
        copy(cown, call.at[s], ca_s.at[t], ca_r.at[s], b, s).wait_recv()

    scaled = jnp.concatenate([call[j] for j in range(nc)], axis=0)
    u = dot3(split(scaled), (ebh, ebl), 1, 1)
    u_sum = reduce_parts(u, usend, urx, uown, uxrx, uall, u_s, u_r)
    for _ in range(3):
        next(u_sum)

    def store_half(h):
        at_half = pl.ds(pl.multiple_of(h * 2 * piece, 2 * piece), 2 * piece)
        upd_v[h] = jnp.concatenate(
            [uall[2 * h + j] - gall[2 * h + j] for j in range(2)], axis=1
        )
        return pltpu.make_async_copy(upd_v.at[h], upd_out.at[:, at_half], out_s.at[1 + h])

    upd_store = store_half(k2)
    upd_store.start()
    next(u_sum)
    upd_last = store_half(1 - k2)
    upd_last.start()

    spread_sent(feat, feat_all, f_s, f_r)

    @pl.loop(1, nc)
    def _(t):
        p_copy(t).wait_send()
        r_copy(t).wait_send()
        c_copy(t).wait_send()
        ca_copy(t).wait_send()

    @pl.loop(0, n - 1)
    def _(t):
        e_copy(t).wait_send()
        o_copy(t).wait_send()

    next(g_sum)
    next(u_sum)
    res_store.wait()
    upd_store.wait()
    upd_last.wait()


def per_device(
    pool_features,
    pool_targets,
    batch_index,
    centers,
    weights,
    eig_vectors,
    eig_scale,
    nys_owner,
    nys_offset,
):
    nb, nc = lax.axis_size("batch"), lax.axis_size("centers")
    n = nb * nc
    rows, (pool, dim) = batch_index.shape[0], pool_features.shape
    outs = pool_targets.shape[1]
    cdev = centers.shape[0]
    pts, q = eig_vectors.shape
    slots = max(2, 2 * pts // nc)
    group, half = 2 * nb, nb // 2
    qb, piece, og = q // nb, cdev // 4, outs // nc
    vm = pltpu.VMEM
    dma = pltpu.SemaphoreType.DMA
    spec = pl.BlockSpec(memory_space=pl.ANY)
    pair = [dma((nc,)), dma((nc,))]
    every = [dma((n,)), dma((n,))]
    sums = [dma((half + 1,)), dma((half + 2,))]
    reduced = [
        vm((4, outs, piece), F32),
        vm((2, outs, piece), F32),
        vm((2, outs, piece), F32),
        vm((half, 2, outs, piece), F32),
        vm((4, outs, piece), F32),
    ]
    residual, update = pl.pallas_call(
        functools.partial(body, nb, nc),
        out_shape=(
            jax.ShapeDtypeStruct((rows, outs), F32),
            jax.ShapeDtypeStruct((outs, cdev), F32),
        ),
        in_specs=[pl.BlockSpec(memory_space=pltpu.HBM)] * 9,
        out_specs=(spec, spec),
        scratch_shapes=[
            vm((pool, dim), F32),
            vm((outs, pool), F32),
            vm((1, rows), jnp.int32),
            pltpu.SMEM((1, rows), jnp.int32),
            vm((cdev, dim), F32),
            vm((outs, cdev), F32),
            vm((pts, q), F32),
            vm((nb, 1, qb), F32),
            vm((1, pts), jnp.int32),
            vm((1, pts), jnp.int32),
            vm((rows, outs), F32),
            vm((2, outs, cdev // 2), F32),
            vm((rows, dim), F32),
            vm((nc, rows, dim), F32),
            vm((cdev, 4 * dim), LOW),
            vm((2 * outs, cdev), LOW),
            vm((nc // 2, 2 * rows, cdev), LOW),
            vm((nc // 2, 2 * rows, cdev), LOW),
            vm((nc, rows // 2, 2 * outs), F32),
            vm((nc, rows // 2, 2 * outs), F32),
            vm((rows // 2, 2 * outs), F32),
            vm((nc, rows // 2, 2 * outs), F32),
            vm((nb, nc * slots, qb), F32),
            vm((n, slots, qb), F32),
            vm((nc, 1, group * slots), F32),
            vm((n, 1, group * slots), F32),
            vm((cdev, qb), F32),
        ]
        + reduced
        + [
            vm((nc, og, qb), F32),
            vm((nc, og, qb), F32),
            vm((og, qb), F32),
            vm((nc, og, qb), F32),
        ]
        + reduced
        + [dma((10,)), dma((3,)), pltpu.SemaphoreType.REGULAR((2,))]
        + pair * 3
        + every * 2
        + sums
        + pair * 2
        + sums,
        compiler_params=pltpu.CompilerParams(
            collective_id=0, has_side_effects=True, vmem_limit_bytes=VMEM
        ),
    )(
        *(
            pltpu.with_memory_space_constraint(array, pltpu.HBM)
            for array in (
                pool_features,
                pool_targets.T,
                batch_index[None, :],
                centers,
                weights.T,
                eig_vectors,
                eig_scale.reshape(nb, 1, qb),
                nys_owner.reshape(1, pts),
                nys_offset[None, :],
            )
        )
    )
    return (residual, update.T)


def solution(mesh):
    placed = (
        P(("batch", "centers"), None),
        P(("batch", "centers"), None),
        P(("batch", "centers")),
        P("centers", None),
        P("centers", None),
        P(("batch", "centers"), None),
        P(),
        P(("batch", "centers"), None),
        P(("batch", "centers")),
    )
    return jax.shard_map(
        per_device,
        mesh=mesh,
        in_specs=placed,
        out_specs=(P(("batch", "centers"), None), P("centers", None)),
        check_vma=False,
    )
```
